32 devices in a mesh: row: 2 (over x), col: 4 (over z), grp: 4 (over y, core).
Axes of the slice: x: 2, y: 2, z: 4, core: 2. Of those that a mesh axis runs over, the one named last changes fastest.
Arguments:
- tokens: bfloat16 [8, 256, 2048], P(('grp', 'row'), None, 'col'), may hold values from -8 to 8
- w_query: bfloat16 [2048, 2048], P(None, 'col'), may hold values from -0.125 to 0.125
- w_key: bfloat16 [2048, 2048], P(None, 'col'), may hold values from -0.125 to 0.125
- w_value: bfloat16 [2048, 2048], P(None, 'col'), may hold values from -0.125 to 0.125
- w_out: bfloat16 [2048, 2048], P('col'), may hold values from -0.125 to 0.125
- diff_lambda: float32 [8], replicated, may hold values from 0.2 to 0.8
- prefix_keys: bfloat16 [8, 4, 256, 2048], P(('grp', 'row'), None, None, 'col'), may hold values from -800 to 800
- prefix_values: bfloat16 [8, 4, 256, 2048], P(('grp', 'row'), None, None, 'col'), may hold values from -6 to 6
- new_len: int32 [8], P(('grp', 'row')), may hold values from 64 to 256
- prefix_len: int32 [8], P(('grp', 'row')), may hold values from 0 to 1024, as said below
- holder: int32 [8, 4], P(('grp', 'row')), may hold values from 0 to 3, as said below
- page_table: int32 [8, 4], replicated, may hold values from 0 to 3, as said below
Outputs:
- hidden: bfloat16 [8, 256, 2048], P(('grp', 'row'), None, 'col')
- page_keys: bfloat16 [4, 2, 4, 64, 2048], P('grp', 'row', None, None, 'col')
- page_values: bfloat16 [4, 2, 4, 64, 2048], P('grp', 'row', None, None, 'col')
The draws below stay inside these ranges and needn't reach their ends.
Inputs may be any that keep to these rules, and one draw needn't show every extreme that they name: `prefix_len`: half of the requests have no prefix; one has exactly 1024. Each row of holder names every group once. For each r and b, the entries page_table[g * 2 + r, b] over the 4 groups g name every slot once.
All inputs are finite; a program needn't handle non-finite values.
Results may differ from the reference program's by a relative error of at most 0.0078.
Values may be sent and summed in bfloat16 or wider, within the bound.
A program may use at most 64 MiB of HBM per device.

```python
import math
import jax
import jax.numpy as jnp
from jax import lax

D = 2048
HEADS = 8
DK = 128
DV = 256
NEWTOK = 256
PMAX = 1024
GROUPS = 4
ROWS = 2
REQS = 8
PAGE = 64
PBLOCK = 256


def draw_tokens(key, part):
    key_base, key_rows = jax.random.split(key, 2)
    base_draw = jax.random.normal(key_base, (REQS, NEWTOK, D), jnp.float32)
    row_scale = jnp.exp(jax.random.uniform(key_rows, (REQS, NEWTOK, 1), jnp.float32, math.log(0.5), math.log(2.0)))
    drawn = base_draw * row_scale
    return jnp.clip(drawn, -8.0, 8.0).astype(jnp.bfloat16)


def draw_prefix_keys(key, part):
    key_base = jax.random.fold_in(key, 0)
    base_draw = jnp.clip(jax.random.normal(key_base, (REQS, GROUPS, PBLOCK, 2 * HEADS * DK), jnp.float32), -8.0, 8.0)
    return base_draw.astype(jnp.bfloat16)


def draw_prefix_len(key, part):
    key_order, key_len = jax.random.split(key, 2)
    shuffled = jax.random.permutation(key_order, REQS)
    lengths = jax.random.randint(key_len, (REQS,), 1, PMAX + 1)
    lengths = lengths.at[shuffled[0]].set(PMAX)
    with_prefix = jnp.zeros((REQS,), jnp.int32).at[shuffled[:REQS // 2]].set(1)
    return jnp.where(with_prefix == 1, lengths, 0).astype(jnp.int32)


def draw_holder(key, part):
    sub_keys = jax.random.split(key, REQS)
    return jax.vmap(lambda sub_key: jax.random.permutation(sub_key, GROUPS))(sub_keys).astype(jnp.int32)


def draw_page_table(key, part):
    sub_keys = jax.random.split(key, ROWS * GROUPS)
    shuffled = jax.vmap(lambda sub_key: jax.random.permutation(sub_key, GROUPS))(sub_keys).reshape(ROWS, GROUPS, GROUPS)
    return jnp.transpose(shuffled, (2, 0, 1)).reshape(REQS, GROUPS).astype(jnp.int32)


def with_ends(entries, rng, low, largest):
    longest = entries.shape.index(max(entries.shape))
    spots = []
    for shift in (0, 1):
        where = [jax.random.randint(jax.random.fold_in(rng, axis), (), 0, length) for axis, length in enumerate(entries.shape)]
        where[longest] = (where[longest] + shift) % entries.shape[longest]
        spots.append(tuple(where))
    return entries.at[spots[0]].set(low).at[spots[1]].set(largest)


def level_of(own_key, shape, pieces, least, top_value):
    factor_of, own = 1.0, jax.random.fold_in(own_key, 6)
    for axis_at, blocks in pieces:
        steps = jnp.exp(jax.random.uniform(jax.random.fold_in(own, axis_at), (blocks,), jnp.float32, least / len(pieces), top_value / len(pieces)))
        factor_of = factor_of * jnp.repeat(steps, shape[axis_at] // blocks).reshape([-1 if axis == axis_at else 1 for axis in range(len(shape))])
    return factor_of


def gaussian(key, shape, scale, reach, cuts=(), kind=jnp.bfloat16):
    entries = jax.random.normal(key, shape, jnp.float32) * scale
    if len(cuts) > 0:
        entries = level_of(key, shape, cuts, -0.22, 0.18) * entries
    return jnp.clip(entries, min=-reach, max=reach).astype(kind)


def setup_inputs(seed: int = 0) -> dict:
    seeds = jax.random.split(jax.random.key(seed), 13)
    return {
        "tokens": draw_tokens(jax.random.fold_in(seeds[12], 71), 0),
        "w_query": gaussian(seeds[1], (D, 2 * HEADS * DK), D ** -0.5, 0.125, ((1, 4),)),
        "w_key": gaussian(seeds[2], (D, 2 * HEADS * DK), D ** -0.5, 0.125, ((1, 4),)),
        "w_value": gaussian(seeds[3], (D, HEADS * DV), D ** -0.5, 0.125, ((1, 4),)),
        "w_out": gaussian(seeds[4], (HEADS * DV, D), (HEADS * DV) ** -0.5, 0.125, ((0, 4),)),
        "diff_lambda": jnp.clip(jax.random.uniform(seeds[5], (HEADS,), jnp.float32, 0.2, 0.8), 0.2, 0.8),
        "prefix_keys": draw_prefix_keys(jax.random.fold_in(seeds[12], 71), 0),
        "prefix_values": gaussian(seeds[7], (REQS, GROUPS, PBLOCK, HEADS * DV), 1.0, 6.0, ((0, 8), (3, 4))),
        "new_len": with_ends(jax.random.randint(seeds[8], (REQS,), NEWTOK // 4, NEWTOK + 1), jax.random.fold_in(seeds[8], 1), NEWTOK // 4, NEWTOK).astype(jnp.int32),
        "prefix_len": draw_prefix_len(jax.random.fold_in(seeds[12], 71), 0),
        "holder": draw_holder(jax.random.fold_in(seeds[12], 71), 0),
        "page_table": draw_page_table(jax.random.fold_in(seeds[12], 71), 0),
    }


EPS_INPUT = 1e-06
EPS_HEAD = 1e-05
OUT_SCALE = 0.8

def head_attend(queries_in, key_set, value_set, allowed):
    scores = jnp.einsum('chd,khd->hck', queries_in.astype(jnp.float32), key_set.astype(jnp.float32), precision=lax.Precision.HIGHEST) * queries_in.shape[-1] ** (-0.5)
    scores = jnp.where(allowed[None], scores, -jnp.inf)
    highest = lax.optimization_barrier(jnp.max(scores, axis=-1, keepdims=True))
    exp_scores = jnp.exp(scores - highest)
    weights = (exp_scores / lax.optimization_barrier(jnp.sum(exp_scores, axis=-1, keepdims=True))).astype(jnp.bfloat16)
    return jnp.einsum('hck,khe->che', weights.astype(jnp.float32), value_set.astype(jnp.float32), precision=lax.Precision.HIGHEST)

def project(flat, inv_rms, weight):
    return (jnp.dot(flat, weight.astype(jnp.float32), precision=lax.Precision.HIGHEST) * inv_rms).astype(jnp.bfloat16)

def reference(tokens, w_query, w_key, w_value, w_out, diff_lambda, prefix_keys, prefix_values, new_len, prefix_len, holder, page_table):
    flat = tokens.reshape(REQS * NEWTOK, D).astype(jnp.float32)
    inv_rms = lax.rsqrt(lax.optimization_barrier(jnp.mean(flat * flat, axis=1, keepdims=True)) + EPS_INPUT)
    queries = project(flat, inv_rms, w_query).reshape(REQS, NEWTOK, HEADS, 2, DK)
    new_keys = project(flat, inv_rms, w_key)
    new_values = project(flat, inv_rms, w_value)
    keys_heads = new_keys.reshape(REQS, NEWTOK, HEADS, 2, DK)
    values_heads = new_values.reshape(REQS, NEWTOK, HEADS, DV)
    request = jnp.arange(REQS, dtype=jnp.int32)
    source = holder * ROWS + (request % ROWS)[:, None]
    asker = jnp.broadcast_to((request // ROWS)[:, None], (REQS, GROUPS))
    fetched_keys = prefix_keys[source, asker].reshape(REQS, PMAX, HEADS, 2, DK)
    fetched_values = prefix_values[source, asker].reshape(REQS, PMAX, HEADS, DV)
    position = jnp.arange(PMAX + NEWTOK, dtype=jnp.int32)
    within = jnp.arange(NEWTOK, dtype=jnp.int32)

    def one_request(index):
        key_set = jnp.concatenate([fetched_keys[index], keys_heads[index]], axis=0)
        value_set = jnp.concatenate([fetched_values[index], values_heads[index]], axis=0)
        allowed = jnp.where(position[None, :] < PMAX, position[None, :] < prefix_len[index], position[None, :] - PMAX <= within[:, None])
        own_queries = queries[index]
        map_zero = head_attend(own_queries[:, :, 0], key_set[:, :, 0], value_set, allowed)
        map_one = head_attend(own_queries[:, :, 1], key_set[:, :, 1], value_set, allowed)
        differ = map_zero - diff_lambda[None, :, None] * map_one
        normed = OUT_SCALE * differ * lax.rsqrt(lax.optimization_barrier(jnp.mean(differ * differ, axis=-1, keepdims=True)) + EPS_HEAD)
        return normed.astype(jnp.bfloat16).reshape(NEWTOK, HEADS * DV)
    attended = lax.map(one_request, request)
    mixed = jnp.dot(attended.reshape(REQS * NEWTOK, HEADS * DV).astype(jnp.float32), w_out.astype(jnp.float32), precision=lax.Precision.HIGHEST)
    is_live = within[None, :] < new_len[:, None]
    summed = tokens.astype(jnp.float32) + mixed.reshape(REQS, NEWTOK, D)
    hidden = jnp.where(is_live[:, :, None], summed, 0.0).astype(jnp.bfloat16)
    table = page_table.reshape(GROUPS, ROWS, GROUPS)
    placed = (table[..., None] == jnp.arange(GROUPS, dtype=jnp.int32)).astype(jnp.float32)

    def to_pages(field, width):
        kept = jnp.where(is_live[:, :, None], field.reshape(REQS, NEWTOK, width).astype(jnp.float32), 0.0)
        blocks = kept.reshape(GROUPS, ROWS, GROUPS, PAGE, width)
        return jnp.einsum('grbs,grbpc->brspc', placed, blocks, precision=lax.Precision.HIGHEST).astype(jnp.bfloat16)
    return (hidden, to_pages(new_keys, 2 * HEADS * DK), to_pages(new_values, HEADS * DV))
```

```python
import functools
import jax
import jax.numpy as jnp
from jax import lax
from jax.experimental import pallas as pl
from jax.experimental.pallas import tpu as pltpu
from jax.sharding import PartitionSpec as P

D = 2048
DK = 128
DV = 256


EPS_INPUT = 1e-06
EPS_HEAD = 1e-05
OUT_SCALE = 0.8


def swapped(x, axis, stride):
    return lax.ppermute(x, axis, [(i, i ^ 1 << stride) for i in range(lax.axis_size(axis))])


def head_attend(queries_in, key_set, value_set, allowed):
    scores = jnp.einsum(
        "chd,khd->hck", queries_in, key_set, preferred_element_type=jnp.float32
    ) * queries_in.shape[-1] ** (-0.5)
    scores = jnp.where(allowed[None], scores, -jnp.inf)
    highest = jnp.max(scores, axis=-1, keepdims=True)
    exp_scores = jnp.exp(scores - highest)
    weights = (exp_scores / jnp.sum(exp_scores, axis=-1, keepdims=True)).astype(jnp.bfloat16)
    return jnp.einsum("hck,khe->che", weights, value_set, preferred_element_type=jnp.float32)


def arrange(is_first, own_part, other_part):
    return (jnp.where(is_first, own_part, other_part), jnp.where(is_first, other_part, own_part))


def head_norm(differ):
    return (
        OUT_SCALE * differ * lax.rsqrt(jnp.mean(differ * differ, axis=-1, keepdims=True) + EPS_HEAD)
    )


MASKED = -1e30
LOG2E = 1.4426950408889634


def fits_kernel(w_query, prefix_keys):
    return w_query.shape[1] % (2 * DK) == 0 and lax.axis_size("grp") == 4 and lax.axis_size("col") == 4


def kernel(
    n_col,
    n_row,
    new_len,
    prefix_len,
    holder,
    page_table,
    diff_lambda,
    tokens,
    w_query,
    w_key,
    w_value,
    w_out,
    prefix_keys,
    prefix_values,
    hidden,
    page_keys,
    page_values,
    tok,
    weights,
    w_last,
    kbuf,
    vbuf,
    sums,
    queries,
    acc,
    top,
    low,
    attended,
    outgoing,
    incoming,
    page_out,
    page_in,
    local_sem,
    tok_send,
    tok_recv,
    pre_send,
    pre_recv,
    page_send,
    page_recv,
    mix_send,
    mix_recv,
):
    groups = 4
    grp = lax.axis_index("grp")
    row = lax.axis_index("row")
    col = lax.axis_index("col")
    slots, cols = tok.shape[1], tok.shape[2]
    heads = queries.shape[1] // (2 * DK)
    block = kbuf.shape[1]
    page = slots // groups
    peers = (None, grp + 1 - 2 * lax.rem(grp, 2), lax.rem(grp + 2, groups), groups - 1 - grp)

    def ahead(step):
        return lax.rem(col + step, n_col)

    def behind(step):
        return lax.rem(col + n_col - step, n_col)

    copies = [
        pltpu.make_async_copy(tokens.at[0], tok.at[0], local_sem.at[0]),
        pltpu.make_async_copy(w_query, weights.at[0], local_sem.at[1]),
        pltpu.make_async_copy(w_key, weights.at[1], local_sem.at[2]),
        pltpu.make_async_copy(w_value, weights.at[2], local_sem.at[3]),
        pltpu.make_async_copy(prefix_keys.at[0, grp], kbuf.at[0], local_sem.at[4]),
        pltpu.make_async_copy(prefix_values.at[0, grp], vbuf.at[0], local_sem.at[5]),
        pltpu.make_async_copy(w_out, w_last, local_sem.at[6]),
    ]
    barrier = pltpu.get_barrier_semaphore()
    for step in range(1, n_col):
        pl.semaphore_signal(
            barrier, inc=1, device_id={"col": ahead(step)}, device_id_type=pl.DeviceIdType.MESH
        )
    for step in range(1, groups):
        pl.semaphore_signal(
            barrier, inc=1, device_id={"grp": peers[step]}, device_id_type=pl.DeviceIdType.MESH
        )
    for copy in copies:
        copy.start()
    pl.semaphore_wait(barrier, n_col - 1 + groups - 1)

    def remote(source, target, send, recv, where):
        return pltpu.make_async_remote_copy(
            src_ref=source,
            dst_ref=target,
            send_sem=send,
            recv_sem=recv,
            device_id=where,
            device_id_type=pl.DeviceIdType.MESH,
        )

    token_copies = [None] + [
        remote(tokens.at[0], tok.at[step], tok_send.at[step], tok_recv.at[step], {"col": ahead(step)})
        for step in range(1, n_col)
    ]
    inner = jnp.logical_and(col > 0, col < n_col - 1)
    forward_to = jnp.where(col == 1, 0, 3)
    forward_slot = jnp.where(col == 1, 1, 3)
    forward = remote(
        tok.at[2], tok.at[forward_slot], tok_send.at[0], tok_recv.at[forward_slot], {"col": forward_to}
    )
    sends_own = {1: col != 3, 2: col >= 0, 3: col != 0}
    for step in (2, 1, 3):
        pl.when(sends_own[step])(token_copies[step].start)
    key_copies, value_copies = [None], [None]
    for step in range(1, groups):
        peer = peers[step]
        key_copies.append(
            remote(
                prefix_keys.at[0, peer], kbuf.at[step], pre_send.at[0, step], pre_recv.at[0, step], {"grp": peer}
            )
        )
        value_copies.append(
            remote(
                prefix_values.at[0, peer], vbuf.at[step], pre_send.at[1, step], pre_recv.at[1, step], {"grp": peer}
            )
        )
    for step in (2, 3, 1):
        key_copies[step].start()
        value_copies[step].start()

    for copy in copies[:4]:
        copy.wait()
    square = jnp.zeros((slots, 1), jnp.float32)
    second = jnp.where(col == 0, 3, 1)
    for turn, step in enumerate((0, 2, second, 4 - second)):
        if turn:
            remote(
                tok.at[step], tok.at[step], tok_send.at[step], tok_recv.at[step], {"col": behind(step)}
            ).wait_recv()
        if turn == 1:
            pl.when(inner)(forward.start)
        shard = tok[step]
        as_float = shard.astype(jnp.float32)
        square = square + jnp.sum(as_float * as_float, axis=1, keepdims=True)
        first = pl.multiple_of(behind(step) * cols, cols)
        for which in range(3):
            part = jnp.dot(
                shard, weights[which, pl.ds(first, cols), :], preferred_element_type=jnp.float32
            )
            if turn:
                part = part + sums[which]
            sums[which] = part
    inv_rms = lax.rsqrt(square / D + EPS_INPUT)
    live = lax.broadcasted_iota(jnp.int32, (slots, 1), 0) < new_len[0]
    queries[...] = (sums[0] * inv_rms).astype(jnp.bfloat16)
    new_keys = (sums[1] * inv_rms).astype(jnp.bfloat16)
    new_values = (sums[2] * inv_rms).astype(jnp.bfloat16)
    kbuf[groups] = new_keys
    vbuf[groups] = new_values
    page_out[0] = jnp.where(live, new_keys, jnp.zeros_like(new_keys))
    page_out[1] = jnp.where(live, new_values, jnp.zeros_like(new_values))

    scale = DK**-0.5 * LOG2E
    key_at = lax.broadcasted_iota(jnp.int32, (slots, block), 1)
    query_at = lax.broadcasted_iota(jnp.int32, (slots, block), 0)

    every = pl.ds(0, slots)
    parts = 2
    tall = slots // parts
    ranges = [pl.ds(part * tall, tall) for part in range(parts)]

    def attend(index, allowed, first, rows):
        for at in range(2 * heads):
            head = at // 2
            scores = lax.dot_general(
                queries[rows, at * DK : (at + 1) * DK],
                kbuf[index, :, at * DK : (at + 1) * DK],
                (((1,), (1,)), ((), ())),
                preferred_element_type=jnp.float32,
            )
            scores = jnp.where(allowed, scores * scale, MASKED)
            highest = jnp.max(scores, axis=1, keepdims=True)
            if not first:
                before = top[at, rows]
                highest = jnp.maximum(before, highest)
            weight = jnp.exp2(scores - highest)
            total = jnp.sum(weight, axis=1, keepdims=True)
            mixed = jnp.dot(
                weight.astype(jnp.bfloat16),
                vbuf[index, :, head * DV : (head + 1) * DV],
                preferred_element_type=jnp.float32,
            )
            if not first:
                decay = jnp.exp2(before - highest)
                total = total + low[at, rows] * decay
                mixed = mixed + acc[at, rows] * decay
            top[at, rows] = highest
            low[at, rows] = total
            acc[at, rows] = mixed

    def share(step, rows):
        first = pl.multiple_of(ahead(step) * cols, cols)
        return jnp.dot(attended[rows, :], w_last[:, pl.ds(first, cols)], preferred_element_type=jnp.float32)

    def valid(step):
        source = peers[step] if step else grp
        place = jnp.int32(0)
        for at in range(groups):
            place = jnp.where(holder[0, at] == source, at, place)
        return prefix_len[0] - place * block

    attend(groups, key_at <= query_at, True, every)
    copies[4].wait()
    copies[5].wait()
    attend(0, key_at < valid(0), False, every)
    for step in range(1, groups - 1):
        key_copies[step].wait_recv()
        value_copies[step].wait_recv()
        attend(step, key_at < valid(step), False, every)
    last = groups - 1
    key_copies[last].wait_recv()
    value_copies[last].wait_recv()
    copies[6].wait()
    key_in_part = lax.broadcasted_iota(jnp.int32, (tall, block), 1)

    crossing = 3 - 2 * lax.rem(col, 2)
    third = 4 - crossing

    def direct(part, step, slot, target):
        return remote(
            outgoing.at[step, ranges[part]],
            incoming.at[slot, ranges[part]],
            mix_send.at[step, part],
            mix_recv.at[slot, part],
            {"col": target},
        )

    def middle(part, relays):
        total = share(2, ranges[part])
        if relays:
            direct(part, 2, 0, ahead(2)).wait_recv()
            total = total + incoming[0, ranges[part]].astype(jnp.float32)
        outgoing[2, ranges[part]] = total.astype(jnp.bfloat16)
        direct(part, 2, 2, ahead(2)).start()

    @pl.when(jnp.logical_not(inner))
    def _():
        incoming[third] = jnp.zeros((slots, cols), jnp.bfloat16)

    for part in range(parts):
        rows = ranges[part]
        attend(last, key_in_part < valid(last), False, rows)
        for head in range(heads):
            zero, one = 2 * head, 2 * head + 1
            differ = acc[zero, rows] * (1.0 / low[zero, rows]) - acc[one, rows] * (
                diff_lambda[col * heads + head] / low[one, rows]
            )
            normed = OUT_SCALE * differ * lax.rsqrt(jnp.mean(differ * differ, axis=1, keepdims=True) + EPS_HEAD)
            attended[rows, head * DV : (head + 1) * DV] = normed.astype(jnp.bfloat16)
        slot = jnp.where(inner, crossing, 0)
        target = jnp.where(inner, ahead(crossing), jnp.where(col == 0, 1, 2))
        outgoing[crossing, rows] = share(crossing, rows).astype(jnp.bfloat16)
        direct(part, crossing, slot, target).start()
        pl.when(jnp.logical_not(inner))(functools.partial(middle, part, False))
        outgoing[third, rows] = share(third, rows).astype(jnp.bfloat16)
        direct(part, third, third, ahead(third)).start()
    for part in range(parts):
        pl.when(inner)(functools.partial(middle, part, True))

    page_copies = []
    for step in range(1, groups):
        peer = peers[step]
        rows = pl.ds(pl.multiple_of(peer * page, page), page)
        for kind in range(2):
            copy = remote(
                page_out.at[kind, rows],
                page_in.at[kind, grp],
                page_send.at[kind, step],
                page_recv.at[kind, step],
                {"grp": peer},
            )
            copy.start()
            page_copies.append(copy)
    for kind in range(2):
        page_in[kind, grp] = page_out[kind, pl.ds(pl.multiple_of(grp * page, page), page), :]

    for copy in page_copies:
        copy.wait_recv()
    for slot in range(groups):
        source = jnp.int32(0)
        for at in range(groups):
            source = jnp.where(page_table[grp, at * n_row + row] == slot, at, source)
        page_keys[0, 0, slot] = page_in[0, source]
        page_values[0, 0, slot] = page_in[1, source]
    for part in range(parts):
        rows = ranges[part]
        total = share(0, rows) + tok[0, rows].astype(jnp.float32)
        pl.when(inner)(direct(part, third, third, ahead(third)).wait_recv)
        for step in (crossing, 2):
            direct(part, step, step, ahead(step)).wait_recv()
        for step in range(1, n_col):
            total = total + incoming[step, rows].astype(jnp.float32)
        at = lax.broadcasted_iota(jnp.int32, (tall, 1), 0) + part * tall
        hidden[0, rows] = jnp.where(at < new_len[0], total, 0.0).astype(jnp.bfloat16)
    for step in range(1, n_col):
        pl.when(sends_own[step])(token_copies[step].wait_send)
    pl.when(inner)(forward.wait_send)
    for copy in key_copies[1:] + value_copies[1:] + page_copies + [direct(part, step, step, ahead(step)) for part in range(parts) for step in range(1, n_col)]:
        copy.wait_send()


def hand_out(*refs):
    sources, results, passing, sems = refs[:3], refs[3:6], refs[6:9], refs[9]
    reads = [pltpu.make_async_copy(sources[at], passing[at], sems.at[0, at]) for at in range(3)]
    writes = [pltpu.make_async_copy(passing[at], results[at], sems.at[1, at]) for at in range(3)]
    for copy in reads:
        copy.start()
    for at in range(3):
        reads[at].wait()
        writes[at].start()
    for copy in writes:
        copy.wait()


def fused(
    tokens,
    w_query,
    w_key,
    w_value,
    w_out,
    diff_lambda,
    prefix_keys,
    prefix_values,
    new_len,
    prefix_len,
    holder,
    page_table,
):
    n_col, n_row, groups = lax.axis_size("col"), lax.axis_size("row"), lax.axis_size("grp")
    slots, cols = tokens.shape[1:]
    depth, wide = w_query.shape
    block = prefix_keys.shape[2]
    page = slots // groups
    maps = wide // DK
    scalars = pl.BlockSpec(memory_space=pltpu.SMEM)
    remains = pl.BlockSpec(memory_space=pltpu.HBM)
    whole = pl.BlockSpec(memory_space=pltpu.VMEM)
    half, full = jnp.bfloat16, jnp.float32
    shapes = ((1, slots, cols), (1, 1, groups, page, wide), (1, 1, groups, page, wide))
    results = tuple(jax.ShapeDtypeStruct(shape, half) for shape in shapes)
    held = pl.pallas_call(
        functools.partial(kernel, n_col, n_row),
        out_shape=results,
        in_specs=[scalars] * 5 + [remains] * 7,
        out_specs=(whole, whole, whole),
        scratch_shapes=[
            pltpu.VMEM((n_col, slots, cols), half),
            pltpu.VMEM((3, depth, wide), half),
            pltpu.VMEM(w_out.shape, half),
            pltpu.VMEM((groups + 1, block, wide), half),
            pltpu.VMEM((groups + 1, block, wide), half),
            pltpu.VMEM((3, slots, wide), full),
            pltpu.VMEM((slots, wide), half),
            pltpu.VMEM((maps, slots, DV), full),
            pltpu.VMEM((maps, slots, 1), full),
            pltpu.VMEM((maps, slots, 1), full),
            pltpu.VMEM((slots, wide), half),
            pltpu.VMEM((n_col, slots, cols), half),
            pltpu.VMEM((n_col, slots, cols), half),
            pltpu.VMEM((2, slots, wide), half),
            pltpu.VMEM((2, groups, page, wide), half),
            pltpu.SemaphoreType.DMA((7,)),
            pltpu.SemaphoreType.DMA((n_col,)),
            pltpu.SemaphoreType.DMA((n_col,)),
            pltpu.SemaphoreType.DMA((2, groups)),
            pltpu.SemaphoreType.DMA((2, groups)),
            pltpu.SemaphoreType.DMA((2, groups)),
            pltpu.SemaphoreType.DMA((2, groups)),
            pltpu.SemaphoreType.DMA((n_col, 2)),
            pltpu.SemaphoreType.DMA((n_col, 2)),
        ],
        compiler_params=pltpu.CompilerParams(
            collective_id=0, has_side_effects=True, vmem_limit_bytes=56 << 20
        ),
    )(
        new_len,
        prefix_len,
        holder,
        page_table.T,
        diff_lambda,
        tokens,
        w_query,
        w_key,
        w_value,
        w_out,
        prefix_keys,
        prefix_values,
    )
    return pl.pallas_call(
        hand_out,
        out_shape=results,
        in_specs=[remains] * 3,
        out_specs=(remains,) * 3,
        scratch_shapes=[pltpu.VMEM(shape, half) for shape in shapes] + [pltpu.SemaphoreType.DMA((2, 3))],
    )(*held)


def local(
    tokens,
    w_query,
    w_key,
    w_value,
    w_out,
    diff_lambda,
    prefix_keys,
    prefix_values,
    new_len,
    prefix_len,
    holder,
    page_table,
):
    if fits_kernel(w_query, prefix_keys):
        return fused(
            tokens,
            w_query,
            w_key,
            w_value,
            w_out,
            diff_lambda,
            prefix_keys,
            prefix_values,
            new_len,
            prefix_len,
            holder,
            page_table,
        )
    groups = lax.axis_size("grp")
    row_count = lax.axis_size("row")
    grp_index = lax.axis_index("grp")
    row_index = lax.axis_index("row")
    col_index = lax.axis_index("col")
    local_tokens = tokens[0]
    slot_count = local_tokens.shape[0]
    query_cols = w_query.shape[1]
    value_cols = w_value.shape[1]
    group_ids = jnp.arange(groups, dtype=jnp.int32)
    got_keys, got_values = (
        lax.all_to_all(prefix_keys[0], "grp", split_axis=0, concat_axis=0, tiled=True),
        lax.all_to_all(prefix_values[0], "grp", split_axis=0, concat_axis=0, tiled=True),
    )
    shard_piece = lax.all_gather(local_tokens, "col", axis=1, tiled=True)

    def partial_product(weight):
        return jnp.dot(shard_piece, weight, preferred_element_type=jnp.float32)

    as_float = shard_piece.astype(jnp.float32)
    query_sum = partial_product(w_query)
    key_sum = partial_product(w_key)
    value_sum = partial_product(w_value)
    square_sum = jnp.sum(as_float * as_float, axis=1)
    inv_rms = lax.rsqrt(square_sum / D + EPS_INPUT)[:, None]
    queries = (query_sum * inv_rms).astype(jnp.bfloat16)
    new_keys = (key_sum * inv_rms).astype(jnp.bfloat16)
    new_values = (value_sum * inv_rms).astype(jnp.bfloat16)
    is_live = jnp.arange(slot_count) < new_len[0]
    zero_entry = jnp.zeros((), jnp.bfloat16)
    page_size = slot_count // groups
    send_keys = jnp.where(is_live[:, None], new_keys, zero_entry).reshape(
        groups, page_size, query_cols
    )
    send_values = jnp.where(is_live[:, None], new_values, zero_entry).reshape(
        groups, page_size, value_cols
    )
    recv_keys, recv_values = (
        lax.all_to_all(send_keys, "grp", split_axis=0, concat_axis=0, tiled=True),
        lax.all_to_all(send_values, "grp", split_axis=0, concat_axis=0, tiled=True),
    )
    pick_block = (holder[0][:, None] == group_ids[None, :]).astype(jnp.bfloat16)
    fetched_keys = (
        jnp.einsum("bh,hpc->bpc", pick_block, got_keys, preferred_element_type=jnp.float32)
        .astype(jnp.bfloat16)
        .reshape(-1, query_cols)
    )
    fetched_values = (
        jnp.einsum("bh,hpc->bpc", pick_block, got_values, preferred_element_type=jnp.float32)
        .astype(jnp.bfloat16)
        .reshape(-1, value_cols)
    )
    prefix_span = fetched_keys.shape[0]
    position = jnp.arange(prefix_span + slot_count)
    within = jnp.arange(slot_count)
    allowed = jnp.where(
        position[None, :] < prefix_span,
        position[None, :] < prefix_len[0],
        position[None, :] - prefix_span <= within[:, None],
    )
    key_own = jnp.concatenate([fetched_keys, new_keys], axis=0)
    value_own = jnp.concatenate([fetched_values, new_values], axis=0)
    if query_cols == DK:
        is_first = col_index % 2 == 0
        head_lam = diff_lambda[col_index // 2]
        half_width = DV // 2
        partner_query, partner_key, partner_value, partner_pkey, partner_pvalue = swapped(
            (queries, new_keys, new_values, fetched_keys, fetched_values), "col", 0
        )
        query_zero, query_one = arrange(is_first, queries, partner_query)
        key_zero, key_one = arrange(
            is_first, key_own, jnp.concatenate([partner_pkey, partner_key], axis=0)
        )
        value_low, value_high = arrange(
            is_first, value_own, jnp.concatenate([partner_pvalue, partner_value], axis=0)
        )
        value_full = jnp.concatenate([value_low, value_high], axis=1)[:, None, :]
        map_zero = head_attend(query_zero[:, None, :], key_zero[:, None, :], value_full, allowed)
        map_one = head_attend(query_one[:, None, :], key_one[:, None, :], value_full, allowed)
        normed = head_norm(map_zero - head_lam * map_one)
        attended = lax.dynamic_slice_in_dim(
            normed[:, 0, :], col_index % 2 * half_width, half_width, 1
        ).astype(jnp.bfloat16)
    else:
        local_heads = query_cols // (2 * DK)
        query_four = queries.reshape(slot_count, local_heads, 2, DK)
        key_four = key_own.reshape(-1, local_heads, 2, DK)
        value_three = value_own.reshape(-1, local_heads, DV)
        map_zero = head_attend(query_four[:, :, 0], key_four[:, :, 0], value_three, allowed)
        map_one = head_attend(query_four[:, :, 1], key_four[:, :, 1], value_three, allowed)
        head_lam = lax.dynamic_slice_in_dim(diff_lambda, col_index * local_heads, local_heads, 0)
        normed = head_norm(map_zero - head_lam[None, :, None] * map_one)
        attended = normed.reshape(slot_count, local_heads * DV).astype(jnp.bfloat16)
    mixed = lax.psum_scatter(
        lax.dot_general(
            w_out, attended, (((0,), (1,)), ((), ())), preferred_element_type=jnp.float32
        ),
        "col",
        scatter_dimension=0,
        tiled=True,
    ).T
    combined = local_tokens.astype(jnp.float32) + mixed
    hidden = jnp.where(is_live[:, None], combined, 0.0).astype(jnp.bfloat16)[None]
    sources = group_ids * row_count + row_index
    slot_of = page_table[sources, grp_index]
    placement_map = (slot_of[None, :] == group_ids[:, None]).astype(jnp.bfloat16)
    page_keys = jnp.einsum(
        "sg,gpc->spc", placement_map, recv_keys, preferred_element_type=jnp.float32
    ).astype(jnp.bfloat16)[None, None]
    page_values = jnp.einsum(
        "sg,gpc->spc", placement_map, recv_values, preferred_element_type=jnp.float32
    ).astype(jnp.bfloat16)[None, None]
    return (hidden, page_keys, page_values)


def solution(mesh):
    placed = (
        P(("grp", "row"), None, "col"),
        P(None, "col"),
        P(None, "col"),
        P(None, "col"),
        P("col", None),
        P(),
        P(("grp", "row"), None, None, "col"),
        P(("grp", "row"), None, None, "col"),
        P(("grp", "row")),
        P(("grp", "row")),
        P(("grp", "row"), None),
        P(),
    )
    return jax.shard_map(
        local,
        mesh=mesh,
        in_specs=placed,
        out_specs=(
            P(("grp", "row"), None, "col"),
            P("grp", "row", None, None, "col"),
            P("grp", "row", None, None, "col"),
        ),
        check_vma=False,
    )
```

```python
import functools
import jax
import jax.numpy as jnp
from jax import lax
from jax.experimental import pallas as pl
from jax.experimental.pallas import tpu as pltpu
from jax.sharding import PartitionSpec as P

D = 2048
DK = 128
DV = 256


EPS_INPUT = 1e-06
EPS_HEAD = 1e-05
OUT_SCALE = 0.8


def swapped(x, axis, stride):
    return lax.ppermute(x, axis, [(i, i ^ 1 << stride) for i in range(lax.axis_size(axis))])


def head_attend(queries_in, key_set, value_set, allowed):
    scores = jnp.einsum(
        "chd,khd->hck", queries_in, key_set, preferred_element_type=jnp.float32
    ) * queries_in.shape[-1] ** (-0.5)
    scores = jnp.where(allowed[None], scores, -jnp.inf)
    highest = jnp.max(scores, axis=-1, keepdims=True)
    exp_scores = jnp.exp(scores - highest)
    weights = (exp_scores / jnp.sum(exp_scores, axis=-1, keepdims=True)).astype(jnp.bfloat16)
    return jnp.einsum("hck,khe->che", weights, value_set, preferred_element_type=jnp.float32)


def arrange(is_first, own_part, other_part):
    return (jnp.where(is_first, own_part, other_part), jnp.where(is_first, other_part, own_part))


def head_norm(differ):
    return (
        OUT_SCALE * differ * lax.rsqrt(jnp.mean(differ * differ, axis=-1, keepdims=True) + EPS_HEAD)
    )


MASKED = -1e30
LOG2E = 1.4426950408889634


def fits_kernel(w_query, prefix_keys):
    sizes = tuple(lax.axis_size(axis) for axis in ("row", "col", "grp"))
    return w_query.shape[1] == 4 * DK and sizes == (2, 4, 4)


def kernel(
    new_len,
    prefix_len,
    holder,
    page_table,
    diff_lambda,
    tokens,
    w_query,
    w_key,
    w_value,
    w_out,
    prefix_keys,
    prefix_values,
    hidden,
    page_keys,
    page_values,
    tok,
    weights,
    kbuf,
    vbuf,
    sums,
    queries,
    attended,
    w_side,
    acc,
    outgoing,
    landed,
    page_out,
    page_in,
    local_sem,
    tok_send,
    tok_recv,
    pre_send,
    pre_recv,
    w_send,
    w_recv,
    across_send,
    across_recv,
    mate_send,
    mate_recv,
    att_send,
    att_recv,
    page_send,
    page_recv,
    last_send,
    last_recv,
):
    groups = 4
    grp = lax.axis_index("grp")
    row = lax.axis_index("row")
    col = lax.axis_index("col")
    slots, cols = tok.shape[1], tok.shape[2]
    heads, block = kbuf.shape[0], kbuf.shape[1] // (groups + 1)
    span = groups * block
    page = slots // groups
    peers = (None, grp + 1 - 2 * lax.rem(grp, 2), lax.rem(grp + 2, groups), groups - 1 - grp)
    mate = peers[1]
    side = col // 2
    partner = col + 1 - 2 * lax.rem(col, 2)
    far_inner = 2 - side
    far_end = 3 - 3 * side
    inner = jnp.logical_and(col > 0, col < 3)
    outer = jnp.logical_not(inner)
    parts = 2
    tall = slots // parts
    ranges = [pl.ds(part * tall, tall) for part in range(parts)]
    others = (partner, far_inner, far_end)

    def head_cols(head):
        return pl.ds(head * DV, DV)

    copies = [
        pltpu.make_async_copy(tokens.at[0], tok.at[col], local_sem.at[0]),
        pltpu.make_async_copy(w_query, weights.at[0], local_sem.at[1]),
        pltpu.make_async_copy(w_key, weights.at[1], local_sem.at[2]),
        pltpu.make_async_copy(w_value, weights.at[2], local_sem.at[3]),
    ]
    own_prefix = [
        [
            pltpu.make_async_copy(
                source.at[0, grp, :, head_cols(head)],
                target.at[head, pl.ds(0, block)],
                local_sem.at[4 + 2 * head + kind],
            )
            for kind, (source, target) in enumerate(((prefix_keys, kbuf), (prefix_values, vbuf)))
        ]
        for head in range(heads)
    ]
    side_cols = pl.ds(pl.multiple_of(side * 2 * cols, 2 * cols), 2 * cols)
    own_w_out = [
        pltpu.make_async_copy(
            w_out.at[pl.ds(head * DV, DV), side_cols], w_side.at[head, col], local_sem.at[8 + head]
        )
        for head in range(heads)
    ]
    barrier = pltpu.get_barrier_semaphore()
    greeted = [{"col": lax.rem(col + step, 4)} for step in range(1, 4)]
    greeted += [{"grp": peers[step]} for step in range(1, groups)]
    greeted += [{"row": 1 - row}]
    for where in greeted:
        pl.semaphore_signal(barrier, inc=1, device_id=where, device_id_type=pl.DeviceIdType.MESH)
    for copy in copies + own_prefix[0] + own_prefix[1] + own_w_out:
        copy.start()
    pl.semaphore_wait(barrier, len(greeted))

    def remote(source, target, send, recv, where):
        return pltpu.make_async_remote_copy(
            src_ref=source,
            dst_ref=target,
            send_sem=send,
            recv_sem=recv,
            device_id=where,
            device_id_type=pl.DeviceIdType.MESH,
        )

    def shard_copy(kind, part, source, target):
        at = tok.at[source, ranges[part]]
        held = tokens.at[0, ranges[part]] if kind < 2 else at
        return remote(held, at, tok_send.at[kind, part], tok_recv.at[source, part], {"col": target})

    own_shards = [
        [shard_copy(0, part, col, partner) for part in range(parts)],
        [shard_copy(1, part, col, far_inner) for part in range(parts)],
    ]
    passed_on = [
        [shard_copy(2 + at, part, source, target) for part in range(parts)]
        for at, (source, target) in enumerate(((partner, far_inner), (far_inner, partner), (far_end, partner)))
    ]
    for part in range(parts):
        own_shards[0][part].start()
        pl.when(inner)(own_shards[1][part].start)

    def prefix_copies(head, step):
        peer = peers[step]
        return [
            remote(
                source.at[0, peer, :, head_cols(head)],
                target.at[head, pl.ds(step * block, block)],
                pre_send.at[kind, head, step],
                pre_recv.at[kind, head, step],
                {"grp": peer},
            )
            for kind, (source, target) in enumerate(((prefix_keys, kbuf), (prefix_values, vbuf)))
        ]

    fetched = [[None] + [prefix_copies(head, step) for step in range(1, groups)] for head in range(heads)]
    for head in range(heads):
        for step in (2, 3, 1):
            for copy in fetched[head][step]:
                copy.start()

    quarter = DV // 4
    quarter_of = 2 * row + lax.rem(grp, 2)
    quarter_across = 2 * (1 - row) + lax.rem(grp, 2)

    def quarter_rows(at):
        return pl.ds(pl.multiple_of(at * quarter, quarter), quarter)

    def w_copy(head, kind, target, target_side):
        return remote(
            w_out.at[
                pl.ds(pl.multiple_of(head * DV + quarter_of * quarter, quarter), quarter),
                pl.ds(pl.multiple_of(target_side * 2 * cols, 2 * cols), 2 * cols),
            ],
            w_side.at[head, col, quarter_rows(quarter_of)],
            w_send.at[kind, head],
            w_recv.at[head, col],
            {"col": target},
        )

    w_far = [w_copy(head, 0, far_inner, 1 - side) for head in range(heads)]
    w_near = [w_copy(head, 1, partner, side) for head in range(heads)]

    def arrived(head, source):
        at = w_side.at[head, source, quarter_rows(quarter_of)]
        return remote(at, at, w_send.at[0, head], w_recv.at[head, source], {"col": far_inner})

    def across(head, kind):
        at = w_side.at[head, others[kind], quarter_rows(quarter_of)]
        return remote(
            at, at, across_send.at[head, kind], across_recv.at[head, others[kind]], {"row": 1 - row}
        )

    def to_mate(head, kind, second):
        at = w_side.at[head, others[kind], quarter_rows(quarter_across if second else quarter_of)]
        return remote(
            at,
            at,
            mate_send.at[head, kind, second],
            mate_recv.at[head, others[kind], second],
            {"grp": mate},
        )

    def spread(head, kind):
        arrived(head, others[kind]).wait_recv()
        across(head, kind).start()
        to_mate(head, kind, 0).start()

    def relay(head, kind):
        across(head, kind).wait_recv()
        to_mate(head, kind, 1).start()

    for copy in copies:
        copy.wait()
    square = jnp.zeros((slots, 1), jnp.float32)
    for turn, source in enumerate((col,) + others):
        if turn:
            for part in range(parts):
                at = tok.at[source, ranges[part]]
                remote(at, at, tok_send.at[0, part], tok_recv.at[source, part], {"col": partner}).wait_recv()
                pl.when(inner)(passed_on[turn - 1][part].start)
        if turn == 1:

            @pl.when(outer)
            def _():
                for copy in w_near:
                    copy.start()

        if turn == 2:
            for copy in w_far:
                copy.start()
        shard = tok[source]
        as_float = shard.astype(jnp.float32)
        square = square + jnp.sum(as_float * as_float, axis=1, keepdims=True)
        first = pl.multiple_of(source * cols, cols)
        for which in range(3):
            part = jnp.dot(
                shard, weights[which, pl.ds(first, cols), :], preferred_element_type=jnp.float32
            )
            if turn:
                part = part + sums[which]
            sums[which] = part
    inv_rms = lax.rsqrt(square / D + EPS_INPUT)
    live = lax.broadcasted_iota(jnp.int32, (slots, 1), 0) < new_len[0]
    queries[...] = (sums[0] * inv_rms).astype(jnp.bfloat16)
    new_keys = (sums[1] * inv_rms).astype(jnp.bfloat16)
    new_values = (sums[2] * inv_rms).astype(jnp.bfloat16)
    for head in range(heads):
        kbuf[head, span : span + slots] = new_keys[:, head * DV : (head + 1) * DV]
        vbuf[head, span : span + slots] = new_values[:, head * DV : (head + 1) * DV]
    page_out[0] = jnp.where(live, new_keys, jnp.zeros_like(new_keys))
    page_out[1] = jnp.where(live, new_values, jnp.zeros_like(new_values))

    scale = DK**-0.5 * LOG2E

    def valid(step):
        source = peers[step] if step else grp
        place = jnp.int32(0)
        for at in range(groups):
            place = jnp.where(holder[0, at] == source, at, place)
        return prefix_len[0] - place * block

    key_at = lax.broadcasted_iota(jnp.int32, (1, block), 1)
    bias = jnp.concatenate(
        [jnp.where(key_at < valid(step), 0.0, MASKED).astype(jnp.float32) for step in range(groups)], axis=1
    )

    def attend(head, part):
        rows = ranges[part]
        maps = []
        causal = lax.broadcasted_iota(jnp.int32, (tall, slots), 1) <= lax.broadcasted_iota(
            jnp.int32, (tall, slots), 0
        ) + part * tall
        for at in range(2):
            asked = queries[rows, (2 * head + at) * DK : (2 * head + at + 1) * DK]
            keys = slice(at * DK, (at + 1) * DK)
            held = lax.dot_general(
                asked, kbuf[head, 0:span, keys], (((1,), (1,)), ((), ())), preferred_element_type=jnp.float32
            )
            fresh = lax.dot_general(
                asked,
                kbuf[head, span : span + slots, keys],
                (((1,), (1,)), ((), ())),
                preferred_element_type=jnp.float32,
            )
            held = held * scale + bias
            fresh = jnp.where(causal, fresh * scale, MASKED)
            highest = jnp.maximum(
                jnp.max(held, axis=1, keepdims=True), jnp.max(fresh, axis=1, keepdims=True)
            )
            held = jnp.exp2(held - highest)
            fresh = jnp.exp2(fresh - highest)
            total = jnp.sum(held, axis=1, keepdims=True) + jnp.sum(fresh, axis=1, keepdims=True)
            mixed = jnp.dot(
                held.astype(jnp.bfloat16), vbuf[head, 0:span], preferred_element_type=jnp.float32
            ) + jnp.dot(
                fresh.astype(jnp.bfloat16),
                vbuf[head, span : span + slots],
                preferred_element_type=jnp.float32,
            )
            maps.append((mixed, total))
        differ = maps[0][0] * (1.0 / maps[0][1]) - maps[1][0] * (
            diff_lambda[col * heads + head] / maps[1][1]
        )
        normed = OUT_SCALE * differ * lax.rsqrt(jnp.mean(differ * differ, axis=1, keepdims=True) + EPS_HEAD)
        attended[head, col, rows] = normed.astype(jnp.bfloat16)

    def hand(head, part, kind, source, target):
        at = attended.at[head, source, ranges[part]]
        return remote(
            at, at, att_send.at[kind, head, part], att_recv.at[head, source, part], {"col": target}
        )

    page_copies = []
    for step in range(1, groups):
        peer = peers[step]
        rows = pl.ds(pl.multiple_of(peer * page, page), page)
        for kind in range(2):
            page_copies.append(
                remote(
                    page_out.at[kind, rows],
                    page_in.at[kind, grp],
                    page_send.at[kind, step],
                    page_recv.at[kind, step],
                    {"grp": peer},
                )
            )

    for head in range(heads):
        for copy in own_prefix[head]:
            copy.wait()
        for step in (1, 2, 3):
            for copy in fetched[head][step]:
                copy.wait_recv()
        if head == heads - 1:
            for copy in page_copies:
                copy.start()
        for part in range(parts):
            attend(head, part)
            hand(head, part, 0, col, far_inner).start()
            pl.when(outer)(hand(head, part, 1, col, partner).start)
        if head == 0:

            @pl.when(inner)
            def _():
                for at in range(heads):
                    spread(at, 0)
                for kind in (1, 2):
                    spread(0, kind)
                for at in range(heads):
                    relay(at, 0)
                for kind in (1, 2):
                    spread(1, kind)


    def last_copy(part):
        return remote(
            outgoing.at[ranges[part]],
            landed.at[ranges[part]],
            last_send.at[part],
            last_recv.at[part],
            {"col": partner},
        )

    def mixed_with(head, part, which):
        first = pl.multiple_of(lax.rem(partner if which == 0 else col, 2) * cols, cols)
        total = None
        for source in range(4):
            term = jnp.dot(
                attended[head, source, ranges[part]],
                w_side[head, source, :, pl.ds(first, cols)],
                preferred_element_type=jnp.float32,
            )
            total = term if total is None else total + term
        return total

    for kind in range(2):
        page_in[kind, grp] = page_out[kind, pl.ds(pl.multiple_of(grp * page, page), page), :]

    @pl.when(inner)
    def _():
        for head in range(heads):
            own_w_out[head].wait()
            for kind in (1, 2):
                relay(head, kind)
            for kind in range(3):
                for second in range(2):
                    to_mate(head, kind, second).wait_recv()
            for part in range(parts):
                rows = ranges[part]
                for source in others:
                    hand(head, part, 0, source, far_inner).wait_recv()
                at = lax.broadcasted_iota(jnp.int32, (tall, 1), 0) + part * tall
                for which, owner in enumerate((partner, col)):
                    total = mixed_with(head, part, which)
                    if head == 0:
                        acc[which, rows] = total + tok[owner, rows].astype(jnp.float32)
                        continue
                    total = jnp.where(at < new_len[0], total + acc[which, rows], 0.0).astype(jnp.bfloat16)
                    if which == 0:
                        outgoing[rows] = total
                        last_copy(part).start()
                    else:
                        hidden[0, rows] = total

    for copy in page_copies:
        copy.wait_recv()
    for slot in range(groups):
        source = jnp.int32(0)
        for at in range(groups):
            source = jnp.where(page_table[grp, at * 2 + row] == slot, at, source)
        page_keys[0, 0, slot] = page_in[0, source]
        page_values[0, 0, slot] = page_in[1, source]

    @pl.when(outer)
    def _():
        for part in range(parts):
            last_copy(part).wait_recv()
            hidden[0, ranges[part]] = landed[ranges[part]]
        own_w_out[0].wait()
        own_w_out[1].wait()
        for copy in w_near:
            copy.wait_send()
        for head in range(heads):
            for part in range(parts):
                hand(head, part, 1, col, partner).wait_send()

    @pl.when(inner)
    def _():
        for copies_of in [own_shards[1]] + passed_on:
            for copy in copies_of:
                copy.wait_send()
        for head in range(heads):
            for kind in range(3):
                across(head, kind).wait_send()
                to_mate(head, kind, 0).wait_send()
                to_mate(head, kind, 1).wait_send()
        for part in range(parts):
            last_copy(part).wait_send()

    for copy in own_shards[0] + w_far + page_copies:
        copy.wait_send()
    for head in range(heads):
        for part in range(parts):
            hand(head, part, 0, col, far_inner).wait_send()
        for step in range(1, groups):
            for copy in fetched[head][step]:
                copy.wait_send()


def hand_out(*refs):
    sources, results, passing, sems = refs[:3], refs[3:6], refs[6:9], refs[9]
    reads = [pltpu.make_async_copy(sources[at], passing[at], sems.at[0, at]) for at in range(3)]
    writes = [pltpu.make_async_copy(passing[at], results[at], sems.at[1, at]) for at in range(3)]
    for copy in reads:
        copy.start()
    for at in range(3):
        reads[at].wait()
        writes[at].start()
    for copy in writes:
        copy.wait()


def fused(
    tokens,
    w_query,
    w_key,
    w_value,
    w_out,
    diff_lambda,
    prefix_keys,
    prefix_values,
    new_len,
    prefix_len,
    holder,
    page_table,
):
    n_col, groups = lax.axis_size("col"), lax.axis_size("grp")
    slots, cols = tokens.shape[1:]
    depth, wide = w_query.shape
    block = prefix_keys.shape[2]
    page = slots // groups
    heads = wide // DV
    scalars = pl.BlockSpec(memory_space=pltpu.SMEM)
    remains = pl.BlockSpec(memory_space=pltpu.HBM)
    whole = pl.BlockSpec(memory_space=pltpu.VMEM)
    half, full = jnp.bfloat16, jnp.float32
    shapes = ((1, slots, cols), (1, 1, groups, page, wide), (1, 1, groups, page, wide))
    results = tuple(jax.ShapeDtypeStruct(shape, half) for shape in shapes)
    held = pl.pallas_call(
        kernel,
        out_shape=results,
        in_specs=[scalars] * 5 + [remains] * 7,
        out_specs=(whole, whole, whole),
        scratch_shapes=[
            pltpu.VMEM((n_col, slots, cols), half),
            pltpu.VMEM((3, depth, wide), half),
            pltpu.VMEM((heads, (groups + 1) * block, DV), half),
            pltpu.VMEM((heads, (groups + 1) * block, DV), half),
            pltpu.VMEM((3, slots, wide), full),
            pltpu.VMEM((slots, wide), half),
            pltpu.VMEM((heads, n_col, slots, DV), half),
            pltpu.VMEM((heads, n_col, DV, 2 * cols), half),
            pltpu.VMEM((2, slots, cols), full),
            pltpu.VMEM((slots, cols), half),
            pltpu.VMEM((slots, cols), half),
            pltpu.VMEM((2, slots, wide), half),
            pltpu.VMEM((2, groups, page, wide), half),
            pltpu.SemaphoreType.DMA((10,)),
            pltpu.SemaphoreType.DMA((5, 2)),
            pltpu.SemaphoreType.DMA((n_col, 2)),
            pltpu.SemaphoreType.DMA((2, heads, groups)),
            pltpu.SemaphoreType.DMA((2, heads, groups)),
            pltpu.SemaphoreType.DMA((2, heads)),
            pltpu.SemaphoreType.DMA((heads, n_col)),
            pltpu.SemaphoreType.DMA((heads, 3)),
            pltpu.SemaphoreType.DMA((heads, n_col)),
            pltpu.SemaphoreType.DMA((heads, 3, 2)),
            pltpu.SemaphoreType.DMA((heads, n_col, 2)),
            pltpu.SemaphoreType.DMA((2, heads, 2)),
            pltpu.SemaphoreType.DMA((heads, n_col, 2)),
            pltpu.SemaphoreType.DMA((2, groups)),
            pltpu.SemaphoreType.DMA((2, groups)),
            pltpu.SemaphoreType.DMA((2,)),
            pltpu.SemaphoreType.DMA((2,)),
        ],
        compiler_params=pltpu.CompilerParams(
            collective_id=0, has_side_effects=True, vmem_limit_bytes=56 << 20
        ),
    )(
        new_len,
        prefix_len,
        holder,
        page_table.T,
        diff_lambda,
        tokens,
        w_query,
        w_key,
        w_value,
        w_out,
        prefix_keys,
        prefix_values,
    )
    return pl.pallas_call(
        hand_out,
        out_shape=results,
        in_specs=[remains] * 3,
        out_specs=(remains,) * 3,
        scratch_shapes=[pltpu.VMEM(shape, half) for shape in shapes] + [pltpu.SemaphoreType.DMA((2, 3))],
    )(*held)


def local(
    tokens,
    w_query,
    w_key,
    w_value,
    w_out,
    diff_lambda,
    prefix_keys,
    prefix_values,
    new_len,
    prefix_len,
    holder,
    page_table,
):
    if fits_kernel(w_query, prefix_keys):
        return fused(
            tokens,
            w_query,
            w_key,
            w_value,
            w_out,
            diff_lambda,
            prefix_keys,
            prefix_values,
            new_len,
            prefix_len,
            holder,
            page_table,
        )
    groups = lax.axis_size("grp")
    row_count = lax.axis_size("row")
    grp_index = lax.axis_index("grp")
    row_index = lax.axis_index("row")
    col_index = lax.axis_index("col")
    local_tokens = tokens[0]
    slot_count = local_tokens.shape[0]
    query_cols = w_query.shape[1]
    value_cols = w_value.shape[1]
    group_ids = jnp.arange(groups, dtype=jnp.int32)
    got_keys, got_values = (
        lax.all_to_all(prefix_keys[0], "grp", split_axis=0, concat_axis=0, tiled=True),
        lax.all_to_all(prefix_values[0], "grp", split_axis=0, concat_axis=0, tiled=True),
    )
    shard_piece = lax.all_gather(local_tokens, "col", axis=1, tiled=True)

    def partial_product(weight):
        return jnp.dot(shard_piece, weight, preferred_element_type=jnp.float32)

    as_float = shard_piece.astype(jnp.float32)
    query_sum = partial_product(w_query)
    key_sum = partial_product(w_key)
    value_sum = partial_product(w_value)
    square_sum = jnp.sum(as_float * as_float, axis=1)
    inv_rms = lax.rsqrt(square_sum / D + EPS_INPUT)[:, None]
    queries = (query_sum * inv_rms).astype(jnp.bfloat16)
    new_keys = (key_sum * inv_rms).astype(jnp.bfloat16)
    new_values = (value_sum * inv_rms).astype(jnp.bfloat16)
    is_live = jnp.arange(slot_count) < new_len[0]
    zero_entry = jnp.zeros((), jnp.bfloat16)
    page_size = slot_count // groups
    send_keys = jnp.where(is_live[:, None], new_keys, zero_entry).reshape(
        groups, page_size, query_cols
    )
    send_values = jnp.where(is_live[:, None], new_values, zero_entry).reshape(
        groups, page_size, value_cols
    )
    recv_keys, recv_values = (
        lax.all_to_all(send_keys, "grp", split_axis=0, concat_axis=0, tiled=True),
        lax.all_to_all(send_values, "grp", split_axis=0, concat_axis=0, tiled=True),
    )
    pick_block = (holder[0][:, None] == group_ids[None, :]).astype(jnp.bfloat16)
    fetched_keys = (
        jnp.einsum("bh,hpc->bpc", pick_block, got_keys, preferred_element_type=jnp.float32)
        .astype(jnp.bfloat16)
        .reshape(-1, query_cols)
    )
    fetched_values = (
        jnp.einsum("bh,hpc->bpc", pick_block, got_values, preferred_element_type=jnp.float32)
        .astype(jnp.bfloat16)
        .reshape(-1, value_cols)
    )
    prefix_span = fetched_keys.shape[0]
    position = jnp.arange(prefix_span + slot_count)
    within = jnp.arange(slot_count)
    allowed = jnp.where(
        position[None, :] < prefix_span,
        position[None, :] < prefix_len[0],
        position[None, :] - prefix_span <= within[:, None],
    )
    key_own = jnp.concatenate([fetched_keys, new_keys], axis=0)
    value_own = jnp.concatenate([fetched_values, new_values], axis=0)
    if query_cols == DK:
        is_first = col_index % 2 == 0
        head_lam = diff_lambda[col_index // 2]
        half_width = DV // 2
        partner_query, partner_key, partner_value, partner_pkey, partner_pvalue = swapped(
            (queries, new_keys, new_values, fetched_keys, fetched_values), "col", 0
        )
        query_zero, query_one = arrange(is_first, queries, partner_query)
        key_zero, key_one = arrange(
            is_first, key_own, jnp.concatenate([partner_pkey, partner_key], axis=0)
        )
        value_low, value_high = arrange(
            is_first, value_own, jnp.concatenate([partner_pvalue, partner_value], axis=0)
        )
        value_full = jnp.concatenate([value_low, value_high], axis=1)[:, None, :]
        map_zero = head_attend(query_zero[:, None, :], key_zero[:, None, :], value_full, allowed)
        map_one = head_attend(query_one[:, None, :], key_one[:, None, :], value_full, allowed)
        normed = head_norm(map_zero - head_lam * map_one)
        attended = lax.dynamic_slice_in_dim(
            normed[:, 0, :], col_index % 2 * half_width, half_width, 1
        ).astype(jnp.bfloat16)
    else:
        local_heads = query_cols // (2 * DK)
        query_four = queries.reshape(slot_count, local_heads, 2, DK)
        key_four = key_own.reshape(-1, local_heads, 2, DK)
        value_three = value_own.reshape(-1, local_heads, DV)
        map_zero = head_attend(query_four[:, :, 0], key_four[:, :, 0], value_three, allowed)
        map_one = head_attend(query_four[:, :, 1], key_four[:, :, 1], value_three, allowed)
        head_lam = lax.dynamic_slice_in_dim(diff_lambda, col_index * local_heads, local_heads, 0)
        normed = head_norm(map_zero - head_lam[None, :, None] * map_one)
        attended = normed.reshape(slot_count, local_heads * DV).astype(jnp.bfloat16)
    mixed = lax.psum_scatter(
        lax.dot_general(
            w_out, attended, (((0,), (1,)), ((), ())), preferred_element_type=jnp.float32
        ),
        "col",
        scatter_dimension=0,
        tiled=True,
    ).T
    combined = local_tokens.astype(jnp.float32) + mixed
    hidden = jnp.where(is_live[:, None], combined, 0.0).astype(jnp.bfloat16)[None]
    sources = group_ids * row_count + row_index
    slot_of = page_table[sources, grp_index]
    placement_map = (slot_of[None, :] == group_ids[:, None]).astype(jnp.bfloat16)
    page_keys = jnp.einsum(
        "sg,gpc->spc", placement_map, recv_keys, preferred_element_type=jnp.float32
    ).astype(jnp.bfloat16)[None, None]
    page_values = jnp.einsum(
        "sg,gpc->spc", placement_map, recv_values, preferred_element_type=jnp.float32
    ).astype(jnp.bfloat16)[None, None]
    return (hidden, page_keys, page_values)


def solution(mesh):
    placed = (
        P(("grp", "row"), None, "col"),
        P(None, "col"),
        P(None, "col"),
        P(None, "col"),
        P("col", None),
        P(),
        P(("grp", "row"), None, None, "col"),
        P(("grp", "row"), None, None, "col"),
        P(("grp", "row")),
        P(("grp", "row")),
        P(("grp", "row"), None),
        P(),
    )
    return jax.shard_map(
        local,
        mesh=mesh,
        in_specs=placed,
        out_specs=(
            P(("grp", "row"), None, "col"),
            P("grp", "row", None, None, "col"),
            P("grp", "row", None, None, "col"),
        ),
        check_vma=False,
    )
```

```python
import functools
import jax
import jax.numpy as jnp
from jax import lax
from jax.experimental import pallas as pl
from jax.experimental.pallas import tpu as pltpu
from jax.sharding import PartitionSpec as P

D = 2048
DK = 128
DV = 256


EPS_INPUT = 1e-06
EPS_HEAD = 1e-05
OUT_SCALE = 0.8


def swapped(x, axis, stride):
    return lax.ppermute(x, axis, [(i, i ^ 1 << stride) for i in range(lax.axis_size(axis))])


def head_attend(queries_in, key_set, value_set, allowed):
    scores = jnp.einsum(
        "chd,khd->hck", queries_in, key_set, preferred_element_type=jnp.float32
    ) * queries_in.shape[-1] ** (-0.5)
    scores = jnp.where(allowed[None], scores, -jnp.inf)
    highest = jnp.max(scores, axis=-1, keepdims=True)
    exp_scores = jnp.exp(scores - highest)
    weights = (exp_scores / jnp.sum(exp_scores, axis=-1, keepdims=True)).astype(jnp.bfloat16)
    return jnp.einsum("hck,khe->che", weights, value_set, preferred_element_type=jnp.float32)


def arrange(is_first, own_part, other_part):
    return (jnp.where(is_first, own_part, other_part), jnp.where(is_first, other_part, own_part))


def head_norm(differ):
    return (
        OUT_SCALE * differ * lax.rsqrt(jnp.mean(differ * differ, axis=-1, keepdims=True) + EPS_HEAD)
    )


MASKED = -1e30
LOG2E = 1.4426950408889634


def fits_kernel(w_query, prefix_keys):
    sizes = tuple(lax.axis_size(axis) for axis in ("row", "col", "grp"))
    return w_query.shape[1] == 4 * DK and sizes == (2, 4, 4)


def kernel(
    new_len_hbm,
    prefix_len_hbm,
    holder_hbm,
    page_table_hbm,
    diff_lambda_hbm,
    tokens,
    w_query,
    w_key,
    w_value,
    w_out,
    prefix_keys,
    prefix_values,
    hidden,
    page_keys,
    page_values,
    tok,
    weights,
    kbuf,
    vbuf,
    sums,
    queries,
    attended,
    w_side,
    acc,
    outgoing,
    landed,
    page_out,
    page_in,
    local_sem,
    tok_send,
    tok_recv,
    pre_send,
    pre_recv,
    w_send,
    w_recv,
    across_send,
    across_recv,
    mate_send,
    mate_recv,
    att_send,
    att_recv,
    page_send,
    page_recv,
    last_send,
    last_recv,
    new_len,
    prefix_len,
    holder,
    page_table,
    diff_lambda,
):
    groups = 4
    grp = lax.axis_index("grp")
    row = lax.axis_index("row")
    col = lax.axis_index("col")
    slots, cols = tok.shape[1], tok.shape[2]
    heads, block = kbuf.shape[0], kbuf.shape[1] // (groups + 1)
    span = groups * block
    page = slots // groups
    peers = (None, grp + 1 - 2 * lax.rem(grp, 2), lax.rem(grp + 2, groups), groups - 1 - grp)
    mate = peers[1]
    side = col // 2
    partner = col + 1 - 2 * lax.rem(col, 2)
    far_inner = 2 - side
    far_end = 3 - 3 * side
    inner = jnp.logical_and(col > 0, col < 3)
    outer = jnp.logical_not(inner)
    parts = 2
    tall = slots // parts
    ranges = [pl.ds(part * tall, tall) for part in range(parts)]
    others = (partner, far_inner, far_end)

    def head_cols(head):
        return pl.ds(head * DV, DV)

    copies = [
        pltpu.make_async_copy(tokens.at[0], tok.at[col], local_sem.at[0]),
        pltpu.make_async_copy(w_query, weights.at[0], local_sem.at[1]),
        pltpu.make_async_copy(w_key, weights.at[1], local_sem.at[2]),
        pltpu.make_async_copy(w_value, weights.at[2], local_sem.at[3]),
    ]
    own_prefix = [
        [
            pltpu.make_async_copy(
                source.at[0, grp, :, head_cols(head)],
                target.at[head, pl.ds(0, block)],
                local_sem.at[4 + 2 * head + kind],
            )
            for kind, (source, target) in enumerate(((prefix_keys, kbuf), (prefix_values, vbuf)))
        ]
        for head in range(heads)
    ]
    side_cols = pl.ds(pl.multiple_of(side * 2 * cols, 2 * cols), 2 * cols)
    own_w_out = [
        pltpu.make_async_copy(
            w_out.at[pl.ds(head * DV, DV), side_cols], w_side.at[head, col], local_sem.at[8 + head]
        )
        for head in range(heads)
    ]
    small = [
        pltpu.make_async_copy(source, target, local_sem.at[10 + at])
        for at, (source, target) in enumerate(
            (
                (new_len_hbm, new_len),
                (prefix_len_hbm, prefix_len),
                (holder_hbm, holder),
                (page_table_hbm, page_table),
                (diff_lambda_hbm, diff_lambda),
            )
        )
    ]
    barrier = pltpu.get_barrier_semaphore()
    greeted = [{"col": lax.rem(col + step, 4)} for step in range(1, 4)]
    greeted += [{"grp": peers[step]} for step in range(1, groups)]
    greeted += [{"row": 1 - row}]
    for where in greeted:
        pl.semaphore_signal(barrier, inc=1, device_id=where, device_id_type=pl.DeviceIdType.MESH)
    for copy in copies + own_prefix[0] + own_prefix[1] + own_w_out + small:
        copy.start()
    pl.semaphore_wait(barrier, len(greeted))

    def remote(source, target, send, recv, where):
        return pltpu.make_async_remote_copy(
            src_ref=source,
            dst_ref=target,
            send_sem=send,
            recv_sem=recv,
            device_id=where,
            device_id_type=pl.DeviceIdType.MESH,
        )

    def shard_copy(kind, part, source, target):
        at = tok.at[source, ranges[part]]
        held = tokens.at[0, ranges[part]] if kind < 2 else at
        return remote(held, at, tok_send.at[kind, part], tok_recv.at[source, part], {"col": target})

    own_shards = [
        [shard_copy(0, part, col, partner) for part in range(parts)],
        [shard_copy(1, part, col, far_inner) for part in range(parts)],
    ]
    passed_on = [
        [shard_copy(2 + at, part, source, target) for part in range(parts)]
        for at, (source, target) in enumerate(((partner, far_inner), (far_inner, partner), (far_end, partner)))
    ]
    for part in range(parts):
        own_shards[0][part].start()
        pl.when(inner)(own_shards[1][part].start)

    def prefix_copies(head, step):
        peer = peers[step]
        return [
            remote(
                source.at[0, peer, :, head_cols(head)],
                target.at[head, pl.ds(step * block, block)],
                pre_send.at[kind, head, step],
                pre_recv.at[kind, head, step],
                {"grp": peer},
            )
            for kind, (source, target) in enumerate(((prefix_keys, kbuf), (prefix_values, vbuf)))
        ]

    fetched = [[None] + [prefix_copies(head, step) for step in range(1, groups)] for head in range(heads)]
    for head in range(heads):
        for step in (2, 3, 1):
            for copy in fetched[head][step]:
                copy.start()

    quarter = DV // 4
    quarter_of = 2 * row + lax.rem(grp, 2)
    quarter_across = 2 * (1 - row) + lax.rem(grp, 2)

    def quarter_rows(at):
        return pl.ds(pl.multiple_of(at * quarter, quarter), quarter)

    def w_copy(head, kind, target, target_side):
        return remote(
            w_out.at[
                pl.ds(pl.multiple_of(head * DV + quarter_of * quarter, quarter), quarter),
                pl.ds(pl.multiple_of(target_side * 2 * cols, 2 * cols), 2 * cols),
            ],
            w_side.at[head, col, quarter_rows(quarter_of)],
            w_send.at[kind, head],
            w_recv.at[head, col],
            {"col": target},
        )

    w_far = [w_copy(head, 0, far_inner, 1 - side) for head in range(heads)]
    half = DV // 2
    core = lax.rem(grp, 2)
    core_half = pl.ds(pl.multiple_of(core * half, half), half)
    w_near = [
        w_copy(0, 1, partner, side),
        remote(
            w_out.at[pl.ds(pl.multiple_of(DV + core * half, half), half), side_cols],
            w_side.at[1, col, core_half],
            w_send.at[1, 1],
            w_recv.at[1, col],
            {"col": partner},
        ),
    ]

    def arrived(head, source):
        at = w_side.at[head, source, quarter_rows(quarter_of)]
        return remote(at, at, w_send.at[0, head], w_recv.at[head, source], {"col": far_inner})

    near_half = w_side.at[1, partner, core_half]
    near_arrived = remote(near_half, near_half, w_send.at[1, 1], w_recv.at[1, partner], {"col": partner})
    near_to_mate = remote(
        near_half, near_half, mate_send.at[1, 0, 0], mate_recv.at[1, partner, 0], {"grp": mate}
    )

    def across(head, kind):
        at = w_side.at[head, others[kind], quarter_rows(quarter_of)]
        return remote(
            at, at, across_send.at[head, kind], across_recv.at[head, others[kind]], {"row": 1 - row}
        )

    def to_mate(head, kind, second):
        at = w_side.at[head, others[kind], quarter_rows(quarter_across if second else quarter_of)]
        return remote(
            at,
            at,
            mate_send.at[head, kind, second],
            mate_recv.at[head, others[kind], second],
            {"grp": mate},
        )

    def spread(head, kind):
        arrived(head, others[kind]).wait_recv()
        across(head, kind).start()
        to_mate(head, kind, 0).start()

    def relay(head, kind):
        across(head, kind).wait_recv()
        to_mate(head, kind, 1).start()

    for copy in copies + small:
        copy.wait()
    square = jnp.zeros((slots, 1), jnp.float32)
    for turn, source in enumerate((col,) + others):
        if turn == 3:
            pl.when(inner)(functools.partial(spread, 0, 0))
        if turn:
            for part in range(parts):
                at = tok.at[source, ranges[part]]
                remote(at, at, tok_send.at[0, part], tok_recv.at[source, part], {"col": partner}).wait_recv()
                pl.when(inner)(passed_on[turn - 1][part].start)
        if turn == 1:

            @pl.when(outer)
            def _():
                for copy in w_near:
                    copy.start()

        if turn >= 2:
            w_far[turn - 2].start()
        shard = tok[source]
        as_float = shard.astype(jnp.float32)
        square = square + jnp.sum(as_float * as_float, axis=1, keepdims=True)
        first = pl.multiple_of(source * cols, cols)
        for which in range(3):
            part = jnp.dot(
                shard, weights[which, pl.ds(first, cols), :], preferred_element_type=jnp.float32
            )
            if turn:
                part = part + sums[which]
            sums[which] = part
    inv_rms = lax.rsqrt(square / D + EPS_INPUT)
    live = lax.broadcasted_iota(jnp.int32, (slots, 1), 0) < new_len[0]
    queries[...] = (sums[0] * inv_rms).astype(jnp.bfloat16)
    new_keys = (sums[1] * inv_rms).astype(jnp.bfloat16)
    new_values = (sums[2] * inv_rms).astype(jnp.bfloat16)
    for head in range(heads):
        kbuf[head, span : span + slots] = new_keys[:, head * DV : (head + 1) * DV]
        vbuf[head, span : span + slots] = new_values[:, head * DV : (head + 1) * DV]
    page_out[0] = jnp.where(live, new_keys, jnp.zeros_like(new_keys))
    page_out[1] = jnp.where(live, new_values, jnp.zeros_like(new_values))

    @pl.when(inner)
    def _():
        spread(0, 1)
        spread(0, 2)

    scale = DK**-0.5 * LOG2E

    def valid(step):
        source = peers[step] if step else grp
        place = jnp.int32(0)
        for at in range(groups):
            place = jnp.where(holder[0, at] == source, at, place)
        return prefix_len[0] - place * block

    key_at = lax.broadcasted_iota(jnp.int32, (1, block), 1)
    bias = jnp.concatenate(
        [jnp.where(key_at < valid(step), 0.0, MASKED).astype(jnp.float32) for step in range(groups)], axis=1
    )

    def attend(head, part):
        rows = ranges[part]
        maps = []
        causal = lax.broadcasted_iota(jnp.int32, (tall, slots), 1) <= lax.broadcasted_iota(
            jnp.int32, (tall, slots), 0
        ) + part * tall
        for at in range(2):
            asked = queries[rows, (2 * head + at) * DK : (2 * head + at + 1) * DK]
            keys = slice(at * DK, (at + 1) * DK)
            held = lax.dot_general(
                asked, kbuf[head, 0:span, keys], (((1,), (1,)), ((), ())), preferred_element_type=jnp.float32
            )
            fresh = lax.dot_general(
                asked,
                kbuf[head, span : span + slots, keys],
                (((1,), (1,)), ((), ())),
                preferred_element_type=jnp.float32,
            )
            held = held * scale + bias
            fresh = jnp.where(causal, fresh * scale, MASKED)
            highest = jnp.maximum(
                jnp.max(held, axis=1, keepdims=True), jnp.max(fresh, axis=1, keepdims=True)
            )
            held = jnp.exp2(held - highest)
            fresh = jnp.exp2(fresh - highest)
            total = jnp.sum(held, axis=1, keepdims=True) + jnp.sum(fresh, axis=1, keepdims=True)
            mixed = jnp.dot(
                held.astype(jnp.bfloat16), vbuf[head, 0:span], preferred_element_type=jnp.float32
            ) + jnp.dot(
                fresh.astype(jnp.bfloat16),
                vbuf[head, span : span + slots],
                preferred_element_type=jnp.float32,
            )
            maps.append((mixed, total))
        differ = maps[0][0] * (1.0 / maps[0][1]) - maps[1][0] * (
            diff_lambda[col * heads + head] / maps[1][1]
        )
        normed = OUT_SCALE * differ * lax.rsqrt(jnp.mean(differ * differ, axis=1, keepdims=True) + EPS_HEAD)
        attended[head, col, rows] = normed.astype(jnp.bfloat16)

    def hand(head, part, kind, source, target):
        at = attended.at[head, source, ranges[part]]
        return remote(
            at, at, att_send.at[kind, head, part], att_recv.at[head, source, part], {"col": target}
        )

    page_copies = []
    for step in range(1, groups):
        peer = peers[step]
        rows = pl.ds(pl.multiple_of(peer * page, page), page)
        for kind in range(2):
            page_copies.append(
                remote(
                    page_out.at[kind, rows],
                    page_in.at[kind, grp],
                    page_send.at[kind, step],
                    page_recv.at[kind, step],
                    {"grp": peer},
                )
            )

    for head in range(heads):
        for copy in own_prefix[head]:
            copy.wait()
        for step in (1, 2, 3):
            for copy in fetched[head][step]:
                copy.wait_recv()
        if head == heads - 1:
            for copy in page_copies:
                copy.start()
        for part in range(parts):
            attend(head, part)
            hand(head, part, 0, col, far_inner).start()
            pl.when(outer)(hand(head, part, 1, col, partner).start)
        if head == 0:

            @pl.when(inner)
            def _():
                spread(1, 1)
                relay(0, 0)
                relay(0, 1)
                near_arrived.wait_recv()
                near_to_mate.start()
                spread(1, 2)
                relay(0, 2)


    def last_copy(part):
        return remote(
            outgoing.at[ranges[part]],
            landed.at[ranges[part]],
            last_send.at[part],
            last_recv.at[part],
            {"col": partner},
        )

    def mixed_with(head, part, which):
        first = pl.multiple_of(lax.rem(partner if which == 0 else col, 2) * cols, cols)
        total = None
        for source in range(4):
            term = jnp.dot(
                attended[head, source, ranges[part]],
                w_side[head, source, :, pl.ds(first, cols)],
                preferred_element_type=jnp.float32,
            )
            total = term if total is None else total + term
        return total

    def mix(head, part, which):
        rows = ranges[part]
        total = mixed_with(head, part, which)
        if head == 0:
            acc[which, rows] = total + tok[partner if which == 0 else col, rows].astype(jnp.float32)
            return
        at = lax.broadcasted_iota(jnp.int32, (tall, 1), 0) + part * tall
        total = jnp.where(at < new_len[0], total + acc[which, rows], 0.0).astype(jnp.bfloat16)
        if which == 0:
            outgoing[rows] = total
            last_copy(part).start()
        else:
            hidden[0, rows] = total

    for kind in range(2):
        page_in[kind, grp] = page_out[kind, pl.ds(pl.multiple_of(grp * page, page), page), :]

    @pl.when(inner)
    def _():
        for head in range(heads):
            own_w_out[head].wait()
            if head:
                relay(1, 1)
                relay(1, 2)
                near_to_mate.wait_recv()
            for kind in range(head, 3):
                for second in range(2):
                    to_mate(head, kind, second).wait_recv()
            for part in range(parts):
                for source in others:
                    hand(head, part, 0, source, far_inner).wait_recv()
                mix(head, part, 0)
            for part in range(parts):
                mix(head, part, 1)

    for copy in page_copies:
        copy.wait_recv()
    for slot in range(groups):
        source = jnp.int32(0)
        for at in range(groups):
            source = jnp.where(page_table[grp, at * 2 + row] == slot, at, source)
        page_keys[0, 0, slot] = page_in[0, source]
        page_values[0, 0, slot] = page_in[1, source]

    @pl.when(outer)
    def _():
        for part in range(parts):
            last_copy(part).wait_recv()
            hidden[0, ranges[part]] = landed[ranges[part]]
        own_w_out[0].wait()
        own_w_out[1].wait()
        for copy in w_near:
            copy.wait_send()
        for head in range(heads):
            for part in range(parts):
                hand(head, part, 1, col, partner).wait_send()

    @pl.when(inner)
    def _():
        for copies_of in [own_shards[1]] + passed_on:
            for copy in copies_of:
                copy.wait_send()
        for head in range(heads):
            for kind in range(head, 3):
                across(head, kind).wait_send()
                to_mate(head, kind, 0).wait_send()
                to_mate(head, kind, 1).wait_send()
        near_to_mate.wait_send()
        for part in range(parts):
            last_copy(part).wait_send()

    for copy in own_shards[0] + w_far + page_copies:
        copy.wait_send()
    for head in range(heads):
        for part in range(parts):
            hand(head, part, 0, col, far_inner).wait_send()
        for step in range(1, groups):
            for copy in fetched[head][step]:
                copy.wait_send()


def fused(
    tokens,
    w_query,
    w_key,
    w_value,
    w_out,
    diff_lambda,
    prefix_keys,
    prefix_values,
    new_len,
    prefix_len,
    holder,
    page_table,
):
    n_col, groups = lax.axis_size("col"), lax.axis_size("grp")
    slots, cols = tokens.shape[1:]
    depth, wide = w_query.shape
    block = prefix_keys.shape[2]
    page = slots // groups
    heads = wide // DV
    remains = pl.BlockSpec(memory_space=pltpu.HBM)
    whole = pl.BlockSpec(memory_space=pltpu.VMEM)
    half, full = jnp.bfloat16, jnp.float32
    shapes = ((1, slots, cols), (1, 1, groups, page, wide), (1, 1, groups, page, wide))
    return pl.pallas_call(
        kernel,
        out_shape=tuple(pltpu.VMEM(shape, half) for shape in shapes),
        in_specs=[remains] * 12,
        out_specs=(whole, whole, whole),
        scratch_shapes=[
            pltpu.VMEM((n_col, slots, cols), half),
            pltpu.VMEM((3, depth, wide), half),
            pltpu.VMEM((heads, (groups + 1) * block, DV), half),
            pltpu.VMEM((heads, (groups + 1) * block, DV), half),
            pltpu.VMEM((3, slots, wide), full),
            pltpu.VMEM((slots, wide), half),
            pltpu.VMEM((heads, n_col, slots, DV), half),
            pltpu.VMEM((heads, n_col, DV, 2 * cols), half),
            pltpu.VMEM((2, slots, cols), full),
            pltpu.VMEM((slots, cols), half),
            pltpu.VMEM((slots, cols), half),
            pltpu.VMEM((2, slots, wide), half),
            pltpu.VMEM((2, groups, page, wide), half),
            pltpu.SemaphoreType.DMA((15,)),
            pltpu.SemaphoreType.DMA((5, 2)),
            pltpu.SemaphoreType.DMA((n_col, 2)),
            pltpu.SemaphoreType.DMA((2, heads, groups)),
            pltpu.SemaphoreType.DMA((2, heads, groups)),
            pltpu.SemaphoreType.DMA((2, heads)),
            pltpu.SemaphoreType.DMA((heads, n_col)),
            pltpu.SemaphoreType.DMA((heads, 3)),
            pltpu.SemaphoreType.DMA((heads, n_col)),
            pltpu.SemaphoreType.DMA((heads, 3, 2)),
            pltpu.SemaphoreType.DMA((heads, n_col, 2)),
            pltpu.SemaphoreType.DMA((2, heads, 2)),
            pltpu.SemaphoreType.DMA((heads, n_col, 2)),
            pltpu.SemaphoreType.DMA((2, groups)),
            pltpu.SemaphoreType.DMA((2, groups)),
            pltpu.SemaphoreType.DMA((2,)),
            pltpu.SemaphoreType.DMA((2,)),
            pltpu.SMEM((1,), jnp.int32),
            pltpu.SMEM((1,), jnp.int32),
            pltpu.SMEM((1, 4), jnp.int32),
            pltpu.SMEM(page_table.shape[::-1], jnp.int32),
            pltpu.SMEM(diff_lambda.shape, full),
        ],
        compiler_params=pltpu.CompilerParams(
            collective_id=0, has_side_effects=True, vmem_limit_bytes=56 << 20
        ),
    )(
        new_len,
        prefix_len,
        holder,
        page_table.T,
        diff_lambda,
        tokens,
        w_query,
        w_key,
        w_value,
        w_out,
        prefix_keys,
        prefix_values,
    )
def local(
    tokens,
    w_query,
    w_key,
    w_value,
    w_out,
    diff_lambda,
    prefix_keys,
    prefix_values,
    new_len,
    prefix_len,
    holder,
    page_table,
):
    if fits_kernel(w_query, prefix_keys):
        return fused(
            tokens,
            w_query,
            w_key,
            w_value,
            w_out,
            diff_lambda,
            prefix_keys,
            prefix_values,
            new_len,
            prefix_len,
            holder,
            page_table,
        )
    groups = lax.axis_size("grp")
    row_count = lax.axis_size("row")
    grp_index = lax.axis_index("grp")
    row_index = lax.axis_index("row")
    col_index = lax.axis_index("col")
    local_tokens = tokens[0]
    slot_count = local_tokens.shape[0]
    query_cols = w_query.shape[1]
    value_cols = w_value.shape[1]
    group_ids = jnp.arange(groups, dtype=jnp.int32)
    got_keys, got_values = (
        lax.all_to_all(prefix_keys[0], "grp", split_axis=0, concat_axis=0, tiled=True),
        lax.all_to_all(prefix_values[0], "grp", split_axis=0, concat_axis=0, tiled=True),
    )
    shard_piece = lax.all_gather(local_tokens, "col", axis=1, tiled=True)

    def partial_product(weight):
        return jnp.dot(shard_piece, weight, preferred_element_type=jnp.float32)

    as_float = shard_piece.astype(jnp.float32)
    query_sum = partial_product(w_query)
    key_sum = partial_product(w_key)
    value_sum = partial_product(w_value)
    square_sum = jnp.sum(as_float * as_float, axis=1)
    inv_rms = lax.rsqrt(square_sum / D + EPS_INPUT)[:, None]
    queries = (query_sum * inv_rms).astype(jnp.bfloat16)
    new_keys = (key_sum * inv_rms).astype(jnp.bfloat16)
    new_values = (value_sum * inv_rms).astype(jnp.bfloat16)
    is_live = jnp.arange(slot_count) < new_len[0]
    zero_entry = jnp.zeros((), jnp.bfloat16)
    page_size = slot_count // groups
    send_keys = jnp.where(is_live[:, None], new_keys, zero_entry).reshape(
        groups, page_size, query_cols
    )
    send_values = jnp.where(is_live[:, None], new_values, zero_entry).reshape(
        groups, page_size, value_cols
    )
    recv_keys, recv_values = (
        lax.all_to_all(send_keys, "grp", split_axis=0, concat_axis=0, tiled=True),
        lax.all_to_all(send_values, "grp", split_axis=0, concat_axis=0, tiled=True),
    )
    pick_block = (holder[0][:, None] == group_ids[None, :]).astype(jnp.bfloat16)
    fetched_keys = (
        jnp.einsum("bh,hpc->bpc", pick_block, got_keys, preferred_element_type=jnp.float32)
        .astype(jnp.bfloat16)
        .reshape(-1, query_cols)
    )
    fetched_values = (
        jnp.einsum("bh,hpc->bpc", pick_block, got_values, preferred_element_type=jnp.float32)
        .astype(jnp.bfloat16)
        .reshape(-1, value_cols)
    )
    prefix_span = fetched_keys.shape[0]
    position = jnp.arange(prefix_span + slot_count)
    within = jnp.arange(slot_count)
    allowed = jnp.where(
        position[None, :] < prefix_span,
        position[None, :] < prefix_len[0],
        position[None, :] - prefix_span <= within[:, None],
    )
    key_own = jnp.concatenate([fetched_keys, new_keys], axis=0)
    value_own = jnp.concatenate([fetched_values, new_values], axis=0)
    if query_cols == DK:
        is_first = col_index % 2 == 0
        head_lam = diff_lambda[col_index // 2]
        half_width = DV // 2
        partner_query, partner_key, partner_value, partner_pkey, partner_pvalue = swapped(
            (queries, new_keys, new_values, fetched_keys, fetched_values), "col", 0
        )
        query_zero, query_one = arrange(is_first, queries, partner_query)
        key_zero, key_one = arrange(
            is_first, key_own, jnp.concatenate([partner_pkey, partner_key], axis=0)
        )
        value_low, value_high = arrange(
            is_first, value_own, jnp.concatenate([partner_pvalue, partner_value], axis=0)
        )
        value_full = jnp.concatenate([value_low, value_high], axis=1)[:, None, :]
        map_zero = head_attend(query_zero[:, None, :], key_zero[:, None, :], value_full, allowed)
        map_one = head_attend(query_one[:, None, :], key_one[:, None, :], value_full, allowed)
        normed = head_norm(map_zero - head_lam * map_one)
        attended = lax.dynamic_slice_in_dim(
            normed[:, 0, :], col_index % 2 * half_width, half_width, 1
        ).astype(jnp.bfloat16)
    else:
        local_heads = query_cols // (2 * DK)
        query_four = queries.reshape(slot_count, local_heads, 2, DK)
        key_four = key_own.reshape(-1, local_heads, 2, DK)
        value_three = value_own.reshape(-1, local_heads, DV)
        map_zero = head_attend(query_four[:, :, 0], key_four[:, :, 0], value_three, allowed)
        map_one = head_attend(query_four[:, :, 1], key_four[:, :, 1], value_three, allowed)
        head_lam = lax.dynamic_slice_in_dim(diff_lambda, col_index * local_heads, local_heads, 0)
        normed = head_norm(map_zero - head_lam[None, :, None] * map_one)
        attended = normed.reshape(slot_count, local_heads * DV).astype(jnp.bfloat16)
    mixed = lax.psum_scatter(
        lax.dot_general(
            w_out, attended, (((0,), (1,)), ((), ())), preferred_element_type=jnp.float32
        ),
        "col",
        scatter_dimension=0,
        tiled=True,
    ).T
    combined = local_tokens.astype(jnp.float32) + mixed
    hidden = jnp.where(is_live[:, None], combined, 0.0).astype(jnp.bfloat16)[None]
    sources = group_ids * row_count + row_index
    slot_of = page_table[sources, grp_index]
    placement_map = (slot_of[None, :] == group_ids[:, None]).astype(jnp.bfloat16)
    page_keys = jnp.einsum(
        "sg,gpc->spc", placement_map, recv_keys, preferred_element_type=jnp.float32
    ).astype(jnp.bfloat16)[None, None]
    page_values = jnp.einsum(
        "sg,gpc->spc", placement_map, recv_values, preferred_element_type=jnp.float32
    ).astype(jnp.bfloat16)[None, None]
    return (hidden, page_keys, page_values)


def solution(mesh):
    placed = (
        P(("grp", "row"), None, "col"),
        P(None, "col"),
        P(None, "col"),
        P(None, "col"),
        P("col", None),
        P(),
        P(("grp", "row"), None, None, "col"),
        P(("grp", "row"), None, None, "col"),
        P(("grp", "row")),
        P(("grp", "row")),
        P(("grp", "row"), None),
        P(),
    )
    return jax.shard_map(
        local,
        mesh=mesh,
        in_specs=placed,
        out_specs=(
            P(("grp", "row"), None, "col"),
            P("grp", "row", None, None, "col"),
            P("grp", "row", None, None, "col"),
        ),
        check_vma=False,
    )
```

```python
import functools
import jax
import jax.numpy as jnp
from jax import lax
from jax.experimental import pallas as pl
from jax.experimental.pallas import tpu as pltpu
from jax.sharding import PartitionSpec as P

D = 2048
DK = 128
DV = 256


EPS_INPUT = 1e-06
EPS_HEAD = 1e-05
OUT_SCALE = 0.8


def swapped(x, axis, stride):
    return lax.ppermute(x, axis, [(i, i ^ 1 << stride) for i in range(lax.axis_size(axis))])


def head_attend(queries_in, key_set, value_set, allowed):
    scores = jnp.einsum(
        "chd,khd->hck", queries_in, key_set, preferred_element_type=jnp.float32
    ) * queries_in.shape[-1] ** (-0.5)
    scores = jnp.where(allowed[None], scores, -jnp.inf)
    highest = jnp.max(scores, axis=-1, keepdims=True)
    exp_scores = jnp.exp(scores - highest)
    weights = (exp_scores / jnp.sum(exp_scores, axis=-1, keepdims=True)).astype(jnp.bfloat16)
    return jnp.einsum("hck,khe->che", weights, value_set, preferred_element_type=jnp.float32)


def arrange(is_first, own_part, other_part):
    return (jnp.where(is_first, own_part, other_part), jnp.where(is_first, other_part, own_part))


def head_norm(differ):
    return (
        OUT_SCALE * differ * lax.rsqrt(jnp.mean(differ * differ, axis=-1, keepdims=True) + EPS_HEAD)
    )


MASKED = -1e30
LOG2E = 1.4426950408889634


def fits_kernel(w_query, prefix_keys):
    sizes = tuple(lax.axis_size(axis) for axis in ("row", "col", "grp"))
    return w_query.shape[1] == 4 * DK and sizes == (2, 4, 4)


def kernel(
    new_len_hbm,
    prefix_len_hbm,
    holder_hbm,
    page_table_hbm,
    diff_lambda_hbm,
    tokens,
    w_query,
    w_key,
    w_value,
    w_out,
    prefix_keys,
    prefix_values,
    result,
    tok,
    weights,
    kbuf,
    vbuf,
    sums,
    queries,
    attended,
    w_side,
    acc,
    outgoing,
    landed,
    page_out,
    page_in,
    local_sem,
    tok_send,
    tok_recv,
    pre_send,
    pre_recv,
    w_send,
    w_recv,
    across_send,
    across_recv,
    mate_send,
    mate_recv,
    att_send,
    att_recv,
    page_send,
    page_recv,
    last_send,
    last_recv,
    new_len,
    prefix_len,
    holder,
    page_table,
    diff_lambda,
):
    groups = 4
    grp = lax.axis_index("grp")
    row = lax.axis_index("row")
    col = lax.axis_index("col")
    slots, cols = tok.shape[1], tok.shape[2]
    heads, block = kbuf.shape[0], kbuf.shape[1] // (groups + 1)
    span = groups * block
    page = slots // groups
    peers = (None, grp + 1 - 2 * lax.rem(grp, 2), lax.rem(grp + 2, groups), groups - 1 - grp)
    mate = peers[1]
    side = col // 2
    partner = col + 1 - 2 * lax.rem(col, 2)
    far_inner = 2 - side
    far_end = 3 - 3 * side
    inner = jnp.logical_and(col > 0, col < 3)
    outer = jnp.logical_not(inner)
    parts = 2
    tall = slots // parts
    ranges = [pl.ds(part * tall, tall) for part in range(parts)]
    others = (partner, far_inner, far_end)

    def head_cols(head):
        return pl.ds(head * DV, DV)

    copies = [
        pltpu.make_async_copy(tokens.at[0], tok.at[col], local_sem.at[0]),
        pltpu.make_async_copy(w_query, weights.at[0], local_sem.at[1]),
        pltpu.make_async_copy(w_key, weights.at[1], local_sem.at[2]),
        pltpu.make_async_copy(w_value, weights.at[2], local_sem.at[3]),
    ]
    own_prefix = [
        [
            pltpu.make_async_copy(
                source.at[0, grp, :, head_cols(head)],
                target.at[head, pl.ds(0, block)],
                local_sem.at[4 + 2 * head + kind],
            )
            for kind, (source, target) in enumerate(((prefix_keys, kbuf), (prefix_values, vbuf)))
        ]
        for head in range(heads)
    ]
    side_cols = pl.ds(pl.multiple_of(side * 2 * cols, 2 * cols), 2 * cols)
    own_w_out = [
        pltpu.make_async_copy(
            w_out.at[pl.ds(head * DV, DV), side_cols], w_side.at[head, col], local_sem.at[8 + head]
        )
        for head in range(heads)
    ]
    small = [
        pltpu.make_async_copy(source, target, local_sem.at[10 + at])
        for at, (source, target) in enumerate(
            (
                (new_len_hbm, new_len),
                (prefix_len_hbm, prefix_len),
                (holder_hbm, holder),
                (page_table_hbm, page_table),
                (diff_lambda_hbm, diff_lambda),
            )
        )
    ]
    barrier = pltpu.get_barrier_semaphore()
    greeted = [{"col": lax.rem(col + step, 4)} for step in range(1, 4)]
    greeted += [{"grp": peers[step]} for step in range(1, groups)]
    greeted += [{"row": 1 - row}]
    for where in greeted:
        pl.semaphore_signal(barrier, inc=1, device_id=where, device_id_type=pl.DeviceIdType.MESH)
    for copy in copies + own_prefix[0] + own_prefix[1] + own_w_out + small:
        copy.start()
    pl.semaphore_wait(barrier, len(greeted))

    def remote(source, target, send, recv, where):
        return pltpu.make_async_remote_copy(
            src_ref=source,
            dst_ref=target,
            send_sem=send,
            recv_sem=recv,
            device_id=where,
            device_id_type=pl.DeviceIdType.MESH,
        )

    def shard_copy(kind, part, source, target):
        at = tok.at[source, ranges[part]]
        held = tokens.at[0, ranges[part]] if kind < 2 else at
        return remote(held, at, tok_send.at[kind, part], tok_recv.at[source, part], {"col": target})

    own_shards = [
        [shard_copy(0, part, col, partner) for part in range(parts)],
        [shard_copy(1, part, col, far_inner) for part in range(parts)],
    ]
    passed_on = [
        [shard_copy(2 + at, part, source, target) for part in range(parts)]
        for at, (source, target) in enumerate(((partner, far_inner), (far_inner, partner), (far_end, partner)))
    ]
    for part in range(parts):
        own_shards[0][part].start()
        pl.when(inner)(own_shards[1][part].start)

    def prefix_copies(head, step):
        peer = peers[step]
        return [
            remote(
                source.at[0, peer, :, head_cols(head)],
                target.at[head, pl.ds(step * block, block)],
                pre_send.at[kind, head, step],
                pre_recv.at[kind, head, step],
                {"grp": peer},
            )
            for kind, (source, target) in enumerate(((prefix_keys, kbuf), (prefix_values, vbuf)))
        ]

    fetched = [[None] + [prefix_copies(head, step) for step in range(1, groups)] for head in range(heads)]
    for head in range(heads):
        for step in (2, 3, 1):
            for copy in fetched[head][step]:
                copy.start()

    quarter = DV // 4
    quarter_of = 2 * row + lax.rem(grp, 2)
    quarter_across = 2 * (1 - row) + lax.rem(grp, 2)

    def quarter_rows(at):
        return pl.ds(pl.multiple_of(at * quarter, quarter), quarter)

    def w_copy(head, kind, target, target_side):
        return remote(
            w_out.at[
                pl.ds(pl.multiple_of(head * DV + quarter_of * quarter, quarter), quarter),
                pl.ds(pl.multiple_of(target_side * 2 * cols, 2 * cols), 2 * cols),
            ],
            w_side.at[head, col, quarter_rows(quarter_of)],
            w_send.at[kind, head],
            w_recv.at[head, col],
            {"col": target},
        )

    w_far = [w_copy(head, 0, far_inner, 1 - side) for head in range(heads)]
    half = DV // 2
    core = lax.rem(grp, 2)
    core_half = pl.ds(pl.multiple_of(core * half, half), half)
    w_near = [
        w_copy(0, 1, partner, side),
        remote(
            w_out.at[pl.ds(pl.multiple_of(DV + core * half, half), half), side_cols],
            w_side.at[1, col, core_half],
            w_send.at[1, 1],
            w_recv.at[1, col],
            {"col": partner},
        ),
    ]

    def arrived(head, source):
        at = w_side.at[head, source, quarter_rows(quarter_of)]
        return remote(at, at, w_send.at[0, head], w_recv.at[head, source], {"col": far_inner})

    near_half = w_side.at[1, partner, core_half]
    near_arrived = remote(near_half, near_half, w_send.at[1, 1], w_recv.at[1, partner], {"col": partner})
    near_to_mate = remote(
        near_half, near_half, mate_send.at[1, 0, 0], mate_recv.at[1, partner, 0], {"grp": mate}
    )

    def across(head, kind):
        at = w_side.at[head, others[kind], quarter_rows(quarter_of)]
        return remote(
            at, at, across_send.at[head, kind], across_recv.at[head, others[kind]], {"row": 1 - row}
        )

    def to_mate(head, kind, second):
        at = w_side.at[head, others[kind], quarter_rows(quarter_across if second else quarter_of)]
        return remote(
            at,
            at,
            mate_send.at[head, kind, second],
            mate_recv.at[head, others[kind], second],
            {"grp": mate},
        )

    def spread(head, kind):
        arrived(head, others[kind]).wait_recv()
        across(head, kind).start()
        to_mate(head, kind, 0).start()

    def relay(head, kind):
        across(head, kind).wait_recv()
        to_mate(head, kind, 1).start()

    for copy in copies + small:
        copy.wait()
    square = jnp.zeros((slots, 1), jnp.float32)
    for turn, source in enumerate((col,) + others):
        if turn == 3:
            pl.when(inner)(functools.partial(spread, 0, 0))
        if turn:
            for part in range(parts):
                at = tok.at[source, ranges[part]]
                remote(at, at, tok_send.at[0, part], tok_recv.at[source, part], {"col": partner}).wait_recv()
                pl.when(inner)(passed_on[turn - 1][part].start)
        if turn == 1:

            @pl.when(outer)
            def _():
                for copy in w_near:
                    copy.start()

        if turn >= 2:
            w_far[turn - 2].start()
        shard = tok[source]
        as_float = shard.astype(jnp.float32)
        square = square + jnp.sum(as_float * as_float, axis=1, keepdims=True)
        first = pl.multiple_of(source * cols, cols)
        for which in range(3):
            part = jnp.dot(
                shard, weights[which, pl.ds(first, cols), :], preferred_element_type=jnp.float32
            )
            if turn:
                part = part + sums[which]
            sums[which] = part
    inv_rms = lax.rsqrt(square / D + EPS_INPUT)
    live = lax.broadcasted_iota(jnp.int32, (slots, 1), 0) < new_len[0]
    queries[...] = (sums[0] * inv_rms).astype(jnp.bfloat16)
    new_keys = (sums[1] * inv_rms).astype(jnp.bfloat16)
    new_values = (sums[2] * inv_rms).astype(jnp.bfloat16)
    for head in range(heads):
        kbuf[head, span : span + slots] = new_keys[:, head * DV : (head + 1) * DV]
        vbuf[head, span : span + slots] = new_values[:, head * DV : (head + 1) * DV]
    page_out[0] = jnp.where(live, new_keys, jnp.zeros_like(new_keys))
    page_out[1] = jnp.where(live, new_values, jnp.zeros_like(new_values))

    @pl.when(inner)
    def _():
        spread(0, 1)
        spread(0, 2)

    scale = DK**-0.5 * LOG2E

    def valid(step):
        source = peers[step] if step else grp
        place = jnp.int32(0)
        for at in range(groups):
            place = jnp.where(holder[0, at] == source, at, place)
        return prefix_len[0] - place * block

    key_at = lax.broadcasted_iota(jnp.int32, (1, block), 1)
    bias = jnp.concatenate(
        [jnp.where(key_at < valid(step), 0.0, MASKED).astype(jnp.float32) for step in range(groups)], axis=1
    )

    def attend(head, part):
        rows = ranges[part]
        maps = []
        causal = lax.broadcasted_iota(jnp.int32, (tall, slots), 1) <= lax.broadcasted_iota(
            jnp.int32, (tall, slots), 0
        ) + part * tall
        for at in range(2):
            asked = queries[rows, (2 * head + at) * DK : (2 * head + at + 1) * DK]
            keys = slice(at * DK, (at + 1) * DK)
            held = lax.dot_general(
                asked, kbuf[head, 0:span, keys], (((1,), (1,)), ((), ())), preferred_element_type=jnp.float32
            )
            fresh = lax.dot_general(
                asked,
                kbuf[head, span : span + slots, keys],
                (((1,), (1,)), ((), ())),
                preferred_element_type=jnp.float32,
            )
            held = held * scale + bias
            fresh = jnp.where(causal, fresh * scale, MASKED)
            highest = jnp.maximum(
                jnp.max(held, axis=1, keepdims=True), jnp.max(fresh, axis=1, keepdims=True)
            )
            held = jnp.exp2(held - highest)
            fresh = jnp.exp2(fresh - highest)
            total = jnp.sum(held, axis=1, keepdims=True) + jnp.sum(fresh, axis=1, keepdims=True)
            mixed = jnp.dot(
                held.astype(jnp.bfloat16), vbuf[head, 0:span], preferred_element_type=jnp.float32
            ) + jnp.dot(
                fresh.astype(jnp.bfloat16),
                vbuf[head, span : span + slots],
                preferred_element_type=jnp.float32,
            )
            maps.append((mixed, total))
        differ = maps[0][0] * (1.0 / maps[0][1]) - maps[1][0] * (
            diff_lambda[col * heads + head] / maps[1][1]
        )
        normed = OUT_SCALE * differ * lax.rsqrt(jnp.mean(differ * differ, axis=1, keepdims=True) + EPS_HEAD)
        attended[head, col, rows] = normed.astype(jnp.bfloat16)

    def hand(head, part, kind, source, target):
        at = attended.at[head, source, ranges[part]]
        return remote(
            at, at, att_send.at[kind, head, part], att_recv.at[head, source, part], {"col": target}
        )

    page_copies = []
    for step in range(1, groups):
        peer = peers[step]
        rows = pl.ds(pl.multiple_of(peer * page, page), page)
        for kind in range(2):
            page_copies.append(
                remote(
                    page_out.at[kind, rows],
                    page_in.at[kind, grp],
                    page_send.at[kind, step],
                    page_recv.at[kind, step],
                    {"grp": peer},
                )
            )

    for head in range(heads):
        for copy in own_prefix[head]:
            copy.wait()
        for step in (1, 2, 3):
            for copy in fetched[head][step]:
                copy.wait_recv()
        if head == heads - 1:
            for copy in page_copies:
                copy.start()
        for part in range(parts):
            attend(head, part)
            hand(head, part, 0, col, far_inner).start()
            pl.when(outer)(hand(head, part, 1, col, partner).start)
        if head == 0:

            @pl.when(inner)
            def _():
                spread(1, 1)
                relay(0, 0)
                relay(0, 1)
                near_arrived.wait_recv()
                near_to_mate.start()
                spread(1, 2)
                relay(0, 2)


    def last_copy(part):
        return remote(
            outgoing.at[ranges[part]],
            landed.at[ranges[part]],
            last_send.at[part],
            last_recv.at[part],
            {"col": partner},
        )

    def mixed_with(head, part, which):
        first = pl.multiple_of(lax.rem(partner if which == 0 else col, 2) * cols, cols)
        total = None
        for source in range(4):
            term = jnp.dot(
                attended[head, source, ranges[part]],
                w_side[head, source, :, pl.ds(first, cols)],
                preferred_element_type=jnp.float32,
            )
            total = term if total is None else total + term
        return total

    def mix(head, part, which):
        rows = ranges[part]
        total = mixed_with(head, part, which)
        if head == 0:
            acc[which, rows] = total + tok[partner if which == 0 else col, rows].astype(jnp.float32)
            return
        at = lax.broadcasted_iota(jnp.int32, (tall, 1), 0) + part * tall
        total = jnp.where(at < new_len[0], total + acc[which, rows], 0.0).astype(jnp.bfloat16)
        if which == 0:
            outgoing[rows] = total
            last_copy(part).start()
        else:
            result[0, rows] = total

    for kind in range(2):
        page_in[kind, grp] = page_out[kind, pl.ds(pl.multiple_of(grp * page, page), page), :]

    @pl.when(inner)
    def _():
        for head in range(heads):
            own_w_out[head].wait()
            if head:
                relay(1, 1)
                relay(1, 2)
                near_to_mate.wait_recv()
            for kind in range(head, 3):
                for second in range(2):
                    to_mate(head, kind, second).wait_recv()
            for part in range(parts):
                for source in others:
                    hand(head, part, 0, source, far_inner).wait_recv()
                mix(head, part, 0)
            for part in range(parts):
                mix(head, part, 1)

    for copy in page_copies:
        copy.wait_recv()
    for slot in range(groups):
        source = jnp.int32(0)
        for at in range(groups):
            source = jnp.where(page_table[grp, at * 2 + row] == slot, at, source)
        for kind in range(2):
            result[1 + kind, slot * page : (slot + 1) * page] = page_in[kind, source]

    @pl.when(outer)
    def _():
        for part in range(parts):
            last_copy(part).wait_recv()
            result[0, ranges[part]] = landed[ranges[part]]
        own_w_out[0].wait()
        own_w_out[1].wait()
        for copy in w_near:
            copy.wait_send()
        for head in range(heads):
            for part in range(parts):
                hand(head, part, 1, col, partner).wait_send()

    @pl.when(inner)
    def _():
        for copies_of in [own_shards[1]] + passed_on:
            for copy in copies_of:
                copy.wait_send()
        for head in range(heads):
            for kind in range(head, 3):
                across(head, kind).wait_send()
                to_mate(head, kind, 0).wait_send()
                to_mate(head, kind, 1).wait_send()
        near_to_mate.wait_send()
        for part in range(parts):
            last_copy(part).wait_send()

    for copy in own_shards[0] + w_far + page_copies:
        copy.wait_send()
    for head in range(heads):
        for part in range(parts):
            hand(head, part, 0, col, far_inner).wait_send()
        for step in range(1, groups):
            for copy in fetched[head][step]:
                copy.wait_send()


def fused(
    tokens,
    w_query,
    w_key,
    w_value,
    w_out,
    diff_lambda,
    prefix_keys,
    prefix_values,
    new_len,
    prefix_len,
    holder,
    page_table,
):
    n_col, groups = lax.axis_size("col"), lax.axis_size("grp")
    slots, cols = tokens.shape[1:]
    depth, wide = w_query.shape
    block = prefix_keys.shape[2]
    page = slots // groups
    heads = wide // DV
    remains = pl.BlockSpec(memory_space=pltpu.HBM)
    whole = pl.BlockSpec(memory_space=pltpu.VMEM)
    half, full = jnp.bfloat16, jnp.float32
    result = pl.pallas_call(
        kernel,
        out_shape=pltpu.VMEM((3, slots, cols), half),
        in_specs=[remains] * 12,
        out_specs=whole,
        scratch_shapes=[
            pltpu.VMEM((n_col, slots, cols), half),
            pltpu.VMEM((3, depth, wide), half),
            pltpu.VMEM((heads, (groups + 1) * block, DV), half),
            pltpu.VMEM((heads, (groups + 1) * block, DV), half),
            pltpu.VMEM((3, slots, wide), full),
            pltpu.VMEM((slots, wide), half),
            pltpu.VMEM((heads, n_col, slots, DV), half),
            pltpu.VMEM((heads, n_col, DV, 2 * cols), half),
            pltpu.VMEM((2, slots, cols), full),
            pltpu.VMEM((slots, cols), half),
            pltpu.VMEM((slots, cols), half),
            pltpu.VMEM((2, slots, wide), half),
            pltpu.VMEM((2, groups, page, wide), half),
            pltpu.SemaphoreType.DMA((15,)),
            pltpu.SemaphoreType.DMA((5, 2)),
            pltpu.SemaphoreType.DMA((n_col, 2)),
            pltpu.SemaphoreType.DMA((2, heads, groups)),
            pltpu.SemaphoreType.DMA((2, heads, groups)),
            pltpu.SemaphoreType.DMA((2, heads)),
            pltpu.SemaphoreType.DMA((heads, n_col)),
            pltpu.SemaphoreType.DMA((heads, 3)),
            pltpu.SemaphoreType.DMA((heads, n_col)),
            pltpu.SemaphoreType.DMA((heads, 3, 2)),
            pltpu.SemaphoreType.DMA((heads, n_col, 2)),
            pltpu.SemaphoreType.DMA((2, heads, 2)),
            pltpu.SemaphoreType.DMA((heads, n_col, 2)),
            pltpu.SemaphoreType.DMA((2, groups)),
            pltpu.SemaphoreType.DMA((2, groups)),
            pltpu.SemaphoreType.DMA((2,)),
            pltpu.SemaphoreType.DMA((2,)),
            pltpu.SMEM((1,), jnp.int32),
            pltpu.SMEM((1,), jnp.int32),
            pltpu.SMEM((1, 4), jnp.int32),
            pltpu.SMEM(page_table.shape[::-1], jnp.int32),
            pltpu.SMEM(diff_lambda.shape, full),
        ],
        compiler_params=pltpu.CompilerParams(
            collective_id=0, has_side_effects=True, vmem_limit_bytes=56 << 20
        ),
    )(
        new_len,
        prefix_len,
        holder,
        page_table.T,
        diff_lambda,
        tokens,
        w_query,
        w_key,
        w_value,
        w_out,
        prefix_keys,
        prefix_values,
    )
    pages = (1, 1, groups, page, wide)
    return result[0:1], result[1].reshape(pages), result[2].reshape(pages)


def local(
    tokens,
    w_query,
    w_key,
    w_value,
    w_out,
    diff_lambda,
    prefix_keys,
    prefix_values,
    new_len,
    prefix_len,
    holder,
    page_table,
):
    if fits_kernel(w_query, prefix_keys):
        return fused(
            tokens,
            w_query,
            w_key,
            w_value,
            w_out,
            diff_lambda,
            prefix_keys,
            prefix_values,
            new_len,
            prefix_len,
            holder,
            page_table,
        )
    groups = lax.axis_size("grp")
    row_count = lax.axis_size("row")
    grp_index = lax.axis_index("grp")
    row_index = lax.axis_index("row")
    col_index = lax.axis_index("col")
    local_tokens = tokens[0]
    slot_count = local_tokens.shape[0]
    query_cols = w_query.shape[1]
    value_cols = w_value.shape[1]
    group_ids = jnp.arange(groups, dtype=jnp.int32)
    got_keys, got_values = (
        lax.all_to_all(prefix_keys[0], "grp", split_axis=0, concat_axis=0, tiled=True),
        lax.all_to_all(prefix_values[0], "grp", split_axis=0, concat_axis=0, tiled=True),
    )
    shard_piece = lax.all_gather(local_tokens, "col", axis=1, tiled=True)

    def partial_product(weight):
        return jnp.dot(shard_piece, weight, preferred_element_type=jnp.float32)

    as_float = shard_piece.astype(jnp.float32)
    query_sum = partial_product(w_query)
    key_sum = partial_product(w_key)
    value_sum = partial_product(w_value)
    square_sum = jnp.sum(as_float * as_float, axis=1)
    inv_rms = lax.rsqrt(square_sum / D + EPS_INPUT)[:, None]
    queries = (query_sum * inv_rms).astype(jnp.bfloat16)
    new_keys = (key_sum * inv_rms).astype(jnp.bfloat16)
    new_values = (value_sum * inv_rms).astype(jnp.bfloat16)
    is_live = jnp.arange(slot_count) < new_len[0]
    zero_entry = jnp.zeros((), jnp.bfloat16)
    page_size = slot_count // groups
    send_keys = jnp.where(is_live[:, None], new_keys, zero_entry).reshape(
        groups, page_size, query_cols
    )
    send_values = jnp.where(is_live[:, None], new_values, zero_entry).reshape(
        groups, page_size, value_cols
    )
    recv_keys, recv_values = (
        lax.all_to_all(send_keys, "grp", split_axis=0, concat_axis=0, tiled=True),
        lax.all_to_all(send_values, "grp", split_axis=0, concat_axis=0, tiled=True),
    )
    pick_block = (holder[0][:, None] == group_ids[None, :]).astype(jnp.bfloat16)
    fetched_keys = (
        jnp.einsum("bh,hpc->bpc", pick_block, got_keys, preferred_element_type=jnp.float32)
        .astype(jnp.bfloat16)
        .reshape(-1, query_cols)
    )
    fetched_values = (
        jnp.einsum("bh,hpc->bpc", pick_block, got_values, preferred_element_type=jnp.float32)
        .astype(jnp.bfloat16)
        .reshape(-1, value_cols)
    )
    prefix_span = fetched_keys.shape[0]
    position = jnp.arange(prefix_span + slot_count)
    within = jnp.arange(slot_count)
    allowed = jnp.where(
        position[None, :] < prefix_span,
        position[None, :] < prefix_len[0],
        position[None, :] - prefix_span <= within[:, None],
    )
    key_own = jnp.concatenate([fetched_keys, new_keys], axis=0)
    value_own = jnp.concatenate([fetched_values, new_values], axis=0)
    if query_cols == DK:
        is_first = col_index % 2 == 0
        head_lam = diff_lambda[col_index // 2]
        half_width = DV // 2
        partner_query, partner_key, partner_value, partner_pkey, partner_pvalue = swapped(
            (queries, new_keys, new_values, fetched_keys, fetched_values), "col", 0
        )
        query_zero, query_one = arrange(is_first, queries, partner_query)
        key_zero, key_one = arrange(
            is_first, key_own, jnp.concatenate([partner_pkey, partner_key], axis=0)
        )
        value_low, value_high = arrange(
            is_first, value_own, jnp.concatenate([partner_pvalue, partner_value], axis=0)
        )
        value_full = jnp.concatenate([value_low, value_high], axis=1)[:, None, :]
        map_zero = head_attend(query_zero[:, None, :], key_zero[:, None, :], value_full, allowed)
        map_one = head_attend(query_one[:, None, :], key_one[:, None, :], value_full, allowed)
        normed = head_norm(map_zero - head_lam * map_one)
        attended = lax.dynamic_slice_in_dim(
            normed[:, 0, :], col_index % 2 * half_width, half_width, 1
        ).astype(jnp.bfloat16)
    else:
        local_heads = query_cols // (2 * DK)
        query_four = queries.reshape(slot_count, local_heads, 2, DK)
        key_four = key_own.reshape(-1, local_heads, 2, DK)
        value_three = value_own.reshape(-1, local_heads, DV)
        map_zero = head_attend(query_four[:, :, 0], key_four[:, :, 0], value_three, allowed)
        map_one = head_attend(query_four[:, :, 1], key_four[:, :, 1], value_three, allowed)
        head_lam = lax.dynamic_slice_in_dim(diff_lambda, col_index * local_heads, local_heads, 0)
        normed = head_norm(map_zero - head_lam[None, :, None] * map_one)
        attended = normed.reshape(slot_count, local_heads * DV).astype(jnp.bfloat16)
    mixed = lax.psum_scatter(
        lax.dot_general(
            w_out, attended, (((0,), (1,)), ((), ())), preferred_element_type=jnp.float32
        ),
        "col",
        scatter_dimension=0,
        tiled=True,
    ).T
    combined = local_tokens.astype(jnp.float32) + mixed
    hidden = jnp.where(is_live[:, None], combined, 0.0).astype(jnp.bfloat16)[None]
    sources = group_ids * row_count + row_index
    slot_of = page_table[sources, grp_index]
    placement_map = (slot_of[None, :] == group_ids[:, None]).astype(jnp.bfloat16)
    page_keys = jnp.einsum(
        "sg,gpc->spc", placement_map, recv_keys, preferred_element_type=jnp.float32
    ).astype(jnp.bfloat16)[None, None]
    page_values = jnp.einsum(
        "sg,gpc->spc", placement_map, recv_values, preferred_element_type=jnp.float32
    ).astype(jnp.bfloat16)[None, None]
    return (hidden, page_keys, page_values)


def solution(mesh):
    placed = (
        P(("grp", "row"), None, "col"),
        P(None, "col"),
        P(None, "col"),
        P(None, "col"),
        P("col", None),
        P(),
        P(("grp", "row"), None, None, "col"),
        P(("grp", "row"), None, None, "col"),
        P(("grp", "row")),
        P(("grp", "row")),
        P(("grp", "row"), None),
        P(),
    )
    return jax.shard_map(
        local,
        mesh=mesh,
        in_specs=placed,
        out_specs=(
            P(("grp", "row"), None, "col"),
            P("grp", "row", None, None, "col"),
            P("grp", "row", None, None, "col"),
        ),
        check_vma=False,
    )
```

```python
import functools
import jax
import jax.numpy as jnp
from jax import lax
from jax.experimental import pallas as pl
from jax.experimental.pallas import tpu as pltpu
from jax.sharding import PartitionSpec as P

D = 2048
DK = 128
DV = 256


EPS_INPUT = 1e-06
EPS_HEAD = 1e-05
OUT_SCALE = 0.8


def swapped(x, axis, stride):
    return lax.ppermute(x, axis, [(i, i ^ 1 << stride) for i in range(lax.axis_size(axis))])


def head_attend(queries_in, key_set, value_set, allowed):
    scores = jnp.einsum(
        "chd,khd->hck", queries_in, key_set, preferred_element_type=jnp.float32
    ) * queries_in.shape[-1] ** (-0.5)
    scores = jnp.where(allowed[None], scores, -jnp.inf)
    highest = jnp.max(scores, axis=-1, keepdims=True)
    exp_scores = jnp.exp(scores - highest)
    weights = (exp_scores / jnp.sum(exp_scores, axis=-1, keepdims=True)).astype(jnp.bfloat16)
    return jnp.einsum("hck,khe->che", weights, value_set, preferred_element_type=jnp.float32)


def arrange(is_first, own_part, other_part):
    return (jnp.where(is_first, own_part, other_part), jnp.where(is_first, other_part, own_part))


def head_norm(differ):
    return (
        OUT_SCALE * differ * lax.rsqrt(jnp.mean(differ * differ, axis=-1, keepdims=True) + EPS_HEAD)
    )


MASKED = -1e30
LOG2E = 1.4426950408889634


def fits_kernel(w_query, prefix_keys):
    sizes = tuple(lax.axis_size(axis) for axis in ("row", "col", "grp"))
    return w_query.shape[1] == 4 * DK and sizes == (2, 4, 4)


def kernel(
    new_len_hbm,
    prefix_len_hbm,
    holder_hbm,
    page_table_hbm,
    diff_lambda_hbm,
    tokens,
    w_query,
    w_key,
    w_value,
    w_out,
    prefix_keys,
    prefix_values,
    result,
    tok,
    weights,
    kbuf,
    vbuf,
    sums,
    queries,
    attended,
    w_side,
    acc,
    outgoing,
    page_out,
    page_in,
    local_sem,
    tok_send,
    tok_recv,
    pre_send,
    pre_recv,
    w_send,
    w_recv,
    across_send,
    across_recv,
    mate_send,
    mate_recv,
    att_send,
    att_recv,
    page_send,
    page_recv,
    last_send,
    last_recv,
    new_len,
    prefix_len,
    holder,
    page_table,
    diff_lambda,
):
    groups = 4
    grp = lax.axis_index("grp")
    row = lax.axis_index("row")
    col = lax.axis_index("col")
    slots, cols = tok.shape[1], tok.shape[2]
    heads, block = kbuf.shape[0], kbuf.shape[1] // (groups + 1)
    span = groups * block
    page = slots // groups
    peers = (None, grp + 1 - 2 * lax.rem(grp, 2), lax.rem(grp + 2, groups), groups - 1 - grp)
    mate = peers[1]
    side = col // 2
    partner = col + 1 - 2 * lax.rem(col, 2)
    far_inner = 2 - side
    far_end = 3 - 3 * side
    inner = jnp.logical_and(col > 0, col < 3)
    outer = jnp.logical_not(inner)
    parts = 2
    tall = slots // parts
    ranges = [pl.ds(part * tall, tall) for part in range(parts)]
    others = (partner, far_inner, far_end)

    def head_cols(head):
        return pl.ds(head * DV, DV)

    copies = [
        pltpu.make_async_copy(tokens.at[0], tok.at[col], local_sem.at[0]),
        pltpu.make_async_copy(w_query, weights.at[0], local_sem.at[1]),
        pltpu.make_async_copy(w_key, weights.at[1], local_sem.at[2]),
        pltpu.make_async_copy(w_value, weights.at[2], local_sem.at[3]),
    ]
    own_prefix = [
        [
            pltpu.make_async_copy(
                source.at[0, grp, :, head_cols(head)],
                target.at[head, pl.ds(0, block)],
                local_sem.at[4 + 2 * head + kind],
            )
            for kind, (source, target) in enumerate(((prefix_keys, kbuf), (prefix_values, vbuf)))
        ]
        for head in range(heads)
    ]
    side_cols = pl.ds(pl.multiple_of(side * 2 * cols, 2 * cols), 2 * cols)
    own_w_out = [
        pltpu.make_async_copy(
            w_out.at[pl.ds(head * DV, DV), side_cols], w_side.at[head, col], local_sem.at[8 + head]
        )
        for head in range(heads)
    ]
    small = [
        pltpu.make_async_copy(source, target, local_sem.at[10 + at])
        for at, (source, target) in enumerate(
            (
                (new_len_hbm, new_len),
                (prefix_len_hbm, prefix_len),
                (holder_hbm, holder),
                (page_table_hbm, page_table),
                (diff_lambda_hbm, diff_lambda),
            )
        )
    ]
    barrier = pltpu.get_barrier_semaphore()
    greeted = [{"col": lax.rem(col + step, 4)} for step in range(1, 4)]
    greeted += [{"grp": peers[step]} for step in range(1, groups)]
    greeted += [{"row": 1 - row}]
    for where in greeted:
        pl.semaphore_signal(barrier, inc=1, device_id=where, device_id_type=pl.DeviceIdType.MESH)
    for copy in copies + own_prefix[0] + own_prefix[1] + own_w_out + small:
        copy.start()
    pl.semaphore_wait(barrier, len(greeted))

    def remote(source, target, send, recv, where):
        return pltpu.make_async_remote_copy(
            src_ref=source,
            dst_ref=target,
            send_sem=send,
            recv_sem=recv,
            device_id=where,
            device_id_type=pl.DeviceIdType.MESH,
        )

    def shard_copy(kind, part, source, target):
        at = tok.at[source, ranges[part]]
        held = tokens.at[0, ranges[part]] if kind < 2 else at
        return remote(held, at, tok_send.at[kind, part], tok_recv.at[source, part], {"col": target})

    own_shards = [
        [shard_copy(0, part, col, partner) for part in range(parts)],
        [shard_copy(1, part, col, far_inner) for part in range(parts)],
    ]
    passed_on = [
        [shard_copy(2 + at, part, source, target) for part in range(parts)]
        for at, (source, target) in enumerate(((partner, far_inner), (far_inner, partner), (far_end, partner)))
    ]
    for part in range(parts):
        own_shards[0][part].start()
        pl.when(inner)(own_shards[1][part].start)

    def prefix_copies(head, step):
        peer = peers[step]
        return [
            remote(
                source.at[0, peer, :, head_cols(head)],
                target.at[head, pl.ds(step * block, block)],
                pre_send.at[kind, head, step],
                pre_recv.at[kind, head, step],
                {"grp": peer},
            )
            for kind, (source, target) in enumerate(((prefix_keys, kbuf), (prefix_values, vbuf)))
        ]

    fetched = [[None] + [prefix_copies(head, step) for step in range(1, groups)] for head in range(heads)]
    for head in range(heads):
        for step in (2, 3, 1):
            for copy in fetched[head][step]:
                copy.start()

    quarter = DV // 4
    quarter_of = 2 * row + lax.rem(grp, 2)
    quarter_across = 2 * (1 - row) + lax.rem(grp, 2)

    def quarter_rows(at):
        return pl.ds(pl.multiple_of(at * quarter, quarter), quarter)

    def w_copy(head, kind, target, target_side):
        return remote(
            w_out.at[
                pl.ds(pl.multiple_of(head * DV + quarter_of * quarter, quarter), quarter),
                pl.ds(pl.multiple_of(target_side * 2 * cols, 2 * cols), 2 * cols),
            ],
            w_side.at[head, col, quarter_rows(quarter_of)],
            w_send.at[kind, head],
            w_recv.at[head, col],
            {"col": target},
        )

    w_far = [w_copy(head, 0, far_inner, 1 - side) for head in range(heads)]
    half = DV // 2
    core = lax.rem(grp, 2)
    core_half = pl.ds(pl.multiple_of(core * half, half), half)
    w_near = [
        w_copy(0, 1, partner, side),
        remote(
            w_out.at[pl.ds(pl.multiple_of(DV + core * half, half), half), side_cols],
            w_side.at[1, col, core_half],
            w_send.at[1, 1],
            w_recv.at[1, col],
            {"col": partner},
        ),
    ]

    def arrived(head, source):
        at = w_side.at[head, source, quarter_rows(quarter_of)]
        return remote(at, at, w_send.at[0, head], w_recv.at[head, source], {"col": far_inner})

    near_half = w_side.at[1, partner, core_half]
    near_arrived = remote(near_half, near_half, w_send.at[1, 1], w_recv.at[1, partner], {"col": partner})
    near_to_mate = remote(
        near_half, near_half, mate_send.at[1, 0, 0], mate_recv.at[1, partner, 0], {"grp": mate}
    )

    def across(head, kind):
        at = w_side.at[head, others[kind], quarter_rows(quarter_of)]
        return remote(
            at, at, across_send.at[head, kind], across_recv.at[head, others[kind]], {"row": 1 - row}
        )

    def to_mate(head, kind, second):
        at = w_side.at[head, others[kind], quarter_rows(quarter_across if second else quarter_of)]
        return remote(
            at,
            at,
            mate_send.at[head, kind, second],
            mate_recv.at[head, others[kind], second],
            {"grp": mate},
        )

    def spread(head, kind):
        arrived(head, others[kind]).wait_recv()
        across(head, kind).start()
        to_mate(head, kind, 0).start()

    def relay(head, kind):
        across(head, kind).wait_recv()
        to_mate(head, kind, 1).start()

    for copy in copies + small:
        copy.wait()
    square = jnp.zeros((slots, 1), jnp.float32)
    for turn, source in enumerate((col,) + others):
        if turn == 3:
            pl.when(inner)(functools.partial(spread, 0, 0))
        if turn:
            for part in range(parts):
                at = tok.at[source, ranges[part]]
                remote(at, at, tok_send.at[0, part], tok_recv.at[source, part], {"col": partner}).wait_recv()
                pl.when(inner)(passed_on[turn - 1][part].start)
        if turn == 1:

            @pl.when(outer)
            def _():
                for copy in w_near:
                    copy.start()

        if turn >= 2:
            w_far[turn - 2].start()
        shard = tok[source]
        as_float = shard.astype(jnp.float32)
        square = square + jnp.sum(as_float * as_float, axis=1, keepdims=True)
        first = pl.multiple_of(source * cols, cols)
        for which in range(3):
            part = jnp.dot(
                shard, weights[which, pl.ds(first, cols), :], preferred_element_type=jnp.float32
            )
            if turn:
                part = part + sums[which]
            sums[which] = part
    inv_rms = lax.rsqrt(square / D + EPS_INPUT)
    live = lax.broadcasted_iota(jnp.int32, (slots, 1), 0) < new_len[0]
    queries[...] = (sums[0] * inv_rms).astype(jnp.bfloat16)
    new_keys = (sums[1] * inv_rms).astype(jnp.bfloat16)
    new_values = (sums[2] * inv_rms).astype(jnp.bfloat16)
    for head in range(heads):
        kbuf[head, span : span + slots] = new_keys[:, head * DV : (head + 1) * DV]
        vbuf[head, span : span + slots] = new_values[:, head * DV : (head + 1) * DV]
    page_out[0] = jnp.where(live, new_keys, jnp.zeros_like(new_keys))
    page_out[1] = jnp.where(live, new_values, jnp.zeros_like(new_values))

    @pl.when(inner)
    def _():
        spread(0, 1)
        spread(0, 2)

    scale = DK**-0.5 * LOG2E

    def valid(step):
        source = peers[step] if step else grp
        place = jnp.int32(0)
        for at in range(groups):
            place = jnp.where(holder[0, at] == source, at, place)
        return prefix_len[0] - place * block

    key_at = lax.broadcasted_iota(jnp.int32, (1, block), 1)
    bias = jnp.concatenate(
        [jnp.where(key_at < valid(step), 0.0, MASKED).astype(jnp.float32) for step in range(groups)], axis=1
    )

    def attend(head, part):
        rows = ranges[part]
        maps = []
        causal = lax.broadcasted_iota(jnp.int32, (tall, slots), 1) <= lax.broadcasted_iota(
            jnp.int32, (tall, slots), 0
        ) + part * tall
        for at in range(2):
            asked = queries[rows, (2 * head + at) * DK : (2 * head + at + 1) * DK]
            keys = slice(at * DK, (at + 1) * DK)
            held = lax.dot_general(
                asked, kbuf[head, 0:span, keys], (((1,), (1,)), ((), ())), preferred_element_type=jnp.float32
            )
            fresh = lax.dot_general(
                asked,
                kbuf[head, span : span + slots, keys],
                (((1,), (1,)), ((), ())),
                preferred_element_type=jnp.float32,
            )
            held = held * scale + bias
            fresh = jnp.where(causal, fresh * scale, MASKED)
            highest = jnp.maximum(
                jnp.max(held, axis=1, keepdims=True), jnp.max(fresh, axis=1, keepdims=True)
            )
            held = jnp.exp2(held - highest)
            fresh = jnp.exp2(fresh - highest)
            total = jnp.sum(held, axis=1, keepdims=True) + jnp.sum(fresh, axis=1, keepdims=True)
            mixed = jnp.dot(
                held.astype(jnp.bfloat16), vbuf[head, 0:span], preferred_element_type=jnp.float32
            ) + jnp.dot(
                fresh.astype(jnp.bfloat16),
                vbuf[head, span : span + slots],
                preferred_element_type=jnp.float32,
            )
            maps.append((mixed, total))
        differ = maps[0][0] * (1.0 / maps[0][1]) - maps[1][0] * (
            diff_lambda[col * heads + head] / maps[1][1]
        )
        normed = OUT_SCALE * differ * lax.rsqrt(jnp.mean(differ * differ, axis=1, keepdims=True) + EPS_HEAD)
        attended[head, col, rows] = normed.astype(jnp.bfloat16)

    def hand(head, part, kind, source, target):
        at = attended.at[head, source, ranges[part]]
        return remote(
            at, at, att_send.at[kind, head, part], att_recv.at[head, source, part], {"col": target}
        )

    page_copies = []
    for step in range(1, groups):
        peer = peers[step]
        rows = pl.ds(pl.multiple_of(peer * page, page), page)
        for kind in range(2):
            page_copies.append(
                remote(
                    page_out.at[kind, rows],
                    page_in.at[kind, grp],
                    page_send.at[kind, step],
                    page_recv.at[kind, step],
                    {"grp": peer},
                )
            )

    for head in range(heads):
        for copy in own_prefix[head]:
            copy.wait()
        for step in (1, 2, 3):
            for copy in fetched[head][step]:
                copy.wait_recv()
        if head == heads - 1:
            for copy in page_copies:
                copy.start()
        for part in range(parts):
            attend(head, part)
            hand(head, part, 0, col, far_inner).start()
            pl.when(outer)(hand(head, part, 1, col, partner).start)
        if head == 0:

            @pl.when(inner)
            def _():
                relay(0, 0)
                spread(1, 1)
                relay(0, 1)
                spread(1, 2)
                near_arrived.wait_recv()
                near_to_mate.start()
                relay(0, 2)
                relay(1, 1)


    def last_copy(part):
        return remote(
            outgoing.at[ranges[part]],
            result.at[0, ranges[part]],
            last_send.at[part],
            last_recv.at[part],
            {"col": partner},
        )

    def mixed_with(head, part, which):
        first = pl.multiple_of(lax.rem(partner if which == 0 else col, 2) * cols, cols)
        total = None
        for source in range(4):
            term = jnp.dot(
                attended[head, source, ranges[part]],
                w_side[head, source, :, pl.ds(first, cols)],
                preferred_element_type=jnp.float32,
            )
            total = term if total is None else total + term
        return total

    def mix(head, part, which):
        rows = ranges[part]
        total = mixed_with(head, part, which)
        if head == 0:
            acc[which, rows] = total + tok[partner if which == 0 else col, rows].astype(jnp.float32)
            return
        at = lax.broadcasted_iota(jnp.int32, (tall, 1), 0) + part * tall
        total = jnp.where(at < new_len[0], total + acc[which, rows], 0.0).astype(jnp.bfloat16)
        if which == 0:
            outgoing[rows] = total
            last_copy(part).start()
        else:
            result[0, rows] = total

    for kind in range(2):
        page_in[kind, grp] = page_out[kind, pl.ds(pl.multiple_of(grp * page, page), page), :]

    @pl.when(inner)
    def _():
        for head in range(heads):
            own_w_out[head].wait()
            if head:
                relay(1, 2)
                near_to_mate.wait_recv()
            for kind in range(head, 3):
                for second in range(2):
                    to_mate(head, kind, second).wait_recv()
            for part in range(parts):
                for source in others:
                    hand(head, part, 0, source, far_inner).wait_recv()
                mix(head, part, 0)
            for part in range(parts):
                mix(head, part, 1)

    for copy in page_copies:
        copy.wait_recv()
    for slot in range(groups):
        source = jnp.int32(0)
        for at in range(groups):
            source = jnp.where(page_table[grp, at * 2 + row] == slot, at, source)
        for kind in range(2):
            result[1 + kind, slot * page : (slot + 1) * page] = page_in[kind, source]

    @pl.when(outer)
    def _():
        for part in range(parts):
            last_copy(part).wait_recv()
        own_w_out[0].wait()
        own_w_out[1].wait()
        for copy in w_near:
            copy.wait_send()
        for head in range(heads):
            for part in range(parts):
                hand(head, part, 1, col, partner).wait_send()

    @pl.when(inner)
    def _():
        for copies_of in [own_shards[1]] + passed_on:
            for copy in copies_of:
                copy.wait_send()
        for head in range(heads):
            for kind in range(head, 3):
                across(head, kind).wait_send()
                to_mate(head, kind, 0).wait_send()
                to_mate(head, kind, 1).wait_send()
        near_to_mate.wait_send()
        for part in range(parts):
            last_copy(part).wait_send()

    for copy in own_shards[0] + w_far + page_copies:
        copy.wait_send()
    for head in range(heads):
        for part in range(parts):
            hand(head, part, 0, col, far_inner).wait_send()
        for step in range(1, groups):
            for copy in fetched[head][step]:
                copy.wait_send()


def fused(
    tokens,
    w_query,
    w_key,
    w_value,
    w_out,
    diff_lambda,
    prefix_keys,
    prefix_values,
    new_len,
    prefix_len,
    holder,
    page_table,
):
    n_col, groups = lax.axis_size("col"), lax.axis_size("grp")
    slots, cols = tokens.shape[1:]
    depth, wide = w_query.shape
    block = prefix_keys.shape[2]
    page = slots // groups
    heads = wide // DV
    remains = pl.BlockSpec(memory_space=pltpu.HBM)
    whole = pl.BlockSpec(memory_space=pltpu.VMEM)
    half, full = jnp.bfloat16, jnp.float32
    result = pl.pallas_call(
        kernel,
        out_shape=pltpu.VMEM((3, slots, cols), half),
        in_specs=[remains] * 12,
        out_specs=whole,
        scratch_shapes=[
            pltpu.VMEM((n_col, slots, cols), half),
            pltpu.VMEM((3, depth, wide), half),
            pltpu.VMEM((heads, (groups + 1) * block, DV), half),
            pltpu.VMEM((heads, (groups + 1) * block, DV), half),
            pltpu.VMEM((3, slots, wide), full),
            pltpu.VMEM((slots, wide), half),
            pltpu.VMEM((heads, n_col, slots, DV), half),
            pltpu.VMEM((heads, n_col, DV, 2 * cols), half),
            pltpu.VMEM((2, slots, cols), full),
            pltpu.VMEM((slots, cols), half),
            pltpu.VMEM((2, slots, wide), half),
            pltpu.VMEM((2, groups, page, wide), half),
            pltpu.SemaphoreType.DMA((15,)),
            pltpu.SemaphoreType.DMA((5, 2)),
            pltpu.SemaphoreType.DMA((n_col, 2)),
            pltpu.SemaphoreType.DMA((2, heads, groups)),
            pltpu.SemaphoreType.DMA((2, heads, groups)),
            pltpu.SemaphoreType.DMA((2, heads)),
            pltpu.SemaphoreType.DMA((heads, n_col)),
            pltpu.SemaphoreType.DMA((heads, 3)),
            pltpu.SemaphoreType.DMA((heads, n_col)),
            pltpu.SemaphoreType.DMA((heads, 3, 2)),
            pltpu.SemaphoreType.DMA((heads, n_col, 2)),
            pltpu.SemaphoreType.DMA((2, heads, 2)),
            pltpu.SemaphoreType.DMA((heads, n_col, 2)),
            pltpu.SemaphoreType.DMA((2, groups)),
            pltpu.SemaphoreType.DMA((2, groups)),
            pltpu.SemaphoreType.DMA((2,)),
            pltpu.SemaphoreType.DMA((2,)),
            pltpu.SMEM((1,), jnp.int32),
            pltpu.SMEM((1,), jnp.int32),
            pltpu.SMEM((1, 4), jnp.int32),
            pltpu.SMEM(page_table.shape[::-1], jnp.int32),
            pltpu.SMEM(diff_lambda.shape, full),
        ],
        compiler_params=pltpu.CompilerParams(
            collective_id=0, has_side_effects=True, vmem_limit_bytes=56 << 20
        ),
    )(
        new_len,
        prefix_len,
        holder,
        page_table.T,
        diff_lambda,
        tokens,
        w_query,
        w_key,
        w_value,
        w_out,
        prefix_keys,
        prefix_values,
    )
    pages = (1, 1, groups, page, wide)
    return result[0:1], result[1].reshape(pages), result[2].reshape(pages)


def local(
    tokens,
    w_query,
    w_key,
    w_value,
    w_out,
    diff_lambda,
    prefix_keys,
    prefix_values,
    new_len,
    prefix_len,
    holder,
    page_table,
):
    if fits_kernel(w_query, prefix_keys):
        return fused(
            tokens,
            w_query,
            w_key,
            w_value,
            w_out,
            diff_lambda,
            prefix_keys,
            prefix_values,
            new_len,
            prefix_len,
            holder,
            page_table,
        )
    groups = lax.axis_size("grp")
    row_count = lax.axis_size("row")
    grp_index = lax.axis_index("grp")
    row_index = lax.axis_index("row")
    col_index = lax.axis_index("col")
    local_tokens = tokens[0]
    slot_count = local_tokens.shape[0]
    query_cols = w_query.shape[1]
    value_cols = w_value.shape[1]
    group_ids = jnp.arange(groups, dtype=jnp.int32)
    got_keys, got_values = (
        lax.all_to_all(prefix_keys[0], "grp", split_axis=0, concat_axis=0, tiled=True),
        lax.all_to_all(prefix_values[0], "grp", split_axis=0, concat_axis=0, tiled=True),
    )
    shard_piece = lax.all_gather(local_tokens, "col", axis=1, tiled=True)

    def partial_product(weight):
        return jnp.dot(shard_piece, weight, preferred_element_type=jnp.float32)

    as_float = shard_piece.astype(jnp.float32)
    query_sum = partial_product(w_query)
    key_sum = partial_product(w_key)
    value_sum = partial_product(w_value)
    square_sum = jnp.sum(as_float * as_float, axis=1)
    inv_rms = lax.rsqrt(square_sum / D + EPS_INPUT)[:, None]
    queries = (query_sum * inv_rms).astype(jnp.bfloat16)
    new_keys = (key_sum * inv_rms).astype(jnp.bfloat16)
    new_values = (value_sum * inv_rms).astype(jnp.bfloat16)
    is_live = jnp.arange(slot_count) < new_len[0]
    zero_entry = jnp.zeros((), jnp.bfloat16)
    page_size = slot_count // groups
    send_keys = jnp.where(is_live[:, None], new_keys, zero_entry).reshape(
        groups, page_size, query_cols
    )
    send_values = jnp.where(is_live[:, None], new_values, zero_entry).reshape(
        groups, page_size, value_cols
    )
    recv_keys, recv_values = (
        lax.all_to_all(send_keys, "grp", split_axis=0, concat_axis=0, tiled=True),
        lax.all_to_all(send_values, "grp", split_axis=0, concat_axis=0, tiled=True),
    )
    pick_block = (holder[0][:, None] == group_ids[None, :]).astype(jnp.bfloat16)
    fetched_keys = (
        jnp.einsum("bh,hpc->bpc", pick_block, got_keys, preferred_element_type=jnp.float32)
        .astype(jnp.bfloat16)
        .reshape(-1, query_cols)
    )
    fetched_values = (
        jnp.einsum("bh,hpc->bpc", pick_block, got_values, preferred_element_type=jnp.float32)
        .astype(jnp.bfloat16)
        .reshape(-1, value_cols)
    )
    prefix_span = fetched_keys.shape[0]
    position = jnp.arange(prefix_span + slot_count)
    within = jnp.arange(slot_count)
    allowed = jnp.where(
        position[None, :] < prefix_span,
        position[None, :] < prefix_len[0],
        position[None, :] - prefix_span <= within[:, None],
    )
    key_own = jnp.concatenate([fetched_keys, new_keys], axis=0)
    value_own = jnp.concatenate([fetched_values, new_values], axis=0)
    if query_cols == DK:
        is_first = col_index % 2 == 0
        head_lam = diff_lambda[col_index // 2]
        half_width = DV // 2
        partner_query, partner_key, partner_value, partner_pkey, partner_pvalue = swapped(
            (queries, new_keys, new_values, fetched_keys, fetched_values), "col", 0
        )
        query_zero, query_one = arrange(is_first, queries, partner_query)
        key_zero, key_one = arrange(
            is_first, key_own, jnp.concatenate([partner_pkey, partner_key], axis=0)
        )
        value_low, value_high = arrange(
            is_first, value_own, jnp.concatenate([partner_pvalue, partner_value], axis=0)
        )
        value_full = jnp.concatenate([value_low, value_high], axis=1)[:, None, :]
        map_zero = head_attend(query_zero[:, None, :], key_zero[:, None, :], value_full, allowed)
        map_one = head_attend(query_one[:, None, :], key_one[:, None, :], value_full, allowed)
        normed = head_norm(map_zero - head_lam * map_one)
        attended = lax.dynamic_slice_in_dim(
            normed[:, 0, :], col_index % 2 * half_width, half_width, 1
        ).astype(jnp.bfloat16)
    else:
        local_heads = query_cols // (2 * DK)
        query_four = queries.reshape(slot_count, local_heads, 2, DK)
        key_four = key_own.reshape(-1, local_heads, 2, DK)
        value_three = value_own.reshape(-1, local_heads, DV)
        map_zero = head_attend(query_four[:, :, 0], key_four[:, :, 0], value_three, allowed)
        map_one = head_attend(query_four[:, :, 1], key_four[:, :, 1], value_three, allowed)
        head_lam = lax.dynamic_slice_in_dim(diff_lambda, col_index * local_heads, local_heads, 0)
        normed = head_norm(map_zero - head_lam[None, :, None] * map_one)
        attended = normed.reshape(slot_count, local_heads * DV).astype(jnp.bfloat16)
    mixed = lax.psum_scatter(
        lax.dot_general(
            w_out, attended, (((0,), (1,)), ((), ())), preferred_element_type=jnp.float32
        ),
        "col",
        scatter_dimension=0,
        tiled=True,
    ).T
    combined = local_tokens.astype(jnp.float32) + mixed
    hidden = jnp.where(is_live[:, None], combined, 0.0).astype(jnp.bfloat16)[None]
    sources = group_ids * row_count + row_index
    slot_of = page_table[sources, grp_index]
    placement_map = (slot_of[None, :] == group_ids[:, None]).astype(jnp.bfloat16)
    page_keys = jnp.einsum(
        "sg,gpc->spc", placement_map, recv_keys, preferred_element_type=jnp.float32
    ).astype(jnp.bfloat16)[None, None]
    page_values = jnp.einsum(
        "sg,gpc->spc", placement_map, recv_values, preferred_element_type=jnp.float32
    ).astype(jnp.bfloat16)[None, None]
    return (hidden, page_keys, page_values)


def solution(mesh):
    placed = (
        P(("grp", "row"), None, "col"),
        P(None, "col"),
        P(None, "col"),
        P(None, "col"),
        P("col", None),
        P(),
        P(("grp", "row"), None, None, "col"),
        P(("grp", "row"), None, None, "col"),
        P(("grp", "row")),
        P(("grp", "row")),
        P(("grp", "row"), None),
        P(),
    )
    return jax.shard_map(
        local,
        mesh=mesh,
        in_specs=placed,
        out_specs=(
            P(("grp", "row"), None, "col"),
            P("grp", "row", None, None, "col"),
            P("grp", "row", None, None, "col"),
        ),
        check_vma=False,
    )
```
